32 devices in a mesh: src: 16 (over z, y, x), lev: 2 (over core).
Axes of the slice: x: 2, y: 2, z: 4, core: 2. Of those that a mesh axis runs over, the one named last changes fastest.
Arguments:
- field: bfloat16 [32768, 256], P('src', 'lev'), may hold values from -6 to 6
- grad_coef: float32 [2, 4, 32768], P(None, None, 'src'), may hold values from -6 to 6
- neighbours: int32 [32768, 4], P('src'), may hold values from 0 to 2175, as said below
- level_weight: float32 [8], replicated, may hold values from 0.2 to 2
- src_index: int32 [2048, 64], P('src'), may hold values from 0 to 2047
- tgt_index: int32 [2048, 32], P('src'), may hold values from 0 to 1023
- block_dest: int32 [2048, 1], P('src'), may hold values from 0 to 15; in each aligned block of 128 rows (0 to 127, 128 to 255, ...) at most 16 rows name the same one
- weights: bfloat16 [2048, 6144], P('src'), may hold values from -0.21875 to 0.21875
Outputs:
- remapped: bfloat16 [16384, 256], P('src', 'lev')
- column_total: float32 [32, 16384], P(None, 'src')
The draws below stay inside these ranges and needn't reach their ends.
Inputs may be any that keep to these rules, and one draw needn't show every extreme that they name: `neighbours`: position 64 + p is the device's own cell p; positions below 64 and from 2112 on are the last and first cells of the devices before and after along the closed curve; a neighbour lies at most 64 cells from the cell. `block_dest`: the 128 blocks of one index of src name one target index at most 16 times.
All inputs are finite; a program needn't handle non-finite values.
Results may differ from the reference program's by a relative error of at most 0.0049.
Values may be sent and summed in bfloat16 or wider, within the bound.
A program may use at most 128 MiB of HBM per device.

```python
import math
import jax
import jax.numpy as jnp
import numpy as np
from jax import lax

FIELDS = 32
LEVELS = 8
K = 4
HW = 64
SB = 64
TB = 32
S_DEV = 2048
T_DEV = 1024
B_DEV = 128
SOURCES = 32768
TARGETS = 16384
BLOCKS = 2048
CAP = 16
COLS = 256
N_SRC = 16


def draw_neighbours(key, part):
    offsets = jax.random.randint(key, (SOURCES, K), -HW, HW + 1)
    position = jnp.arange(SOURCES, dtype=jnp.int32) % S_DEV
    first_column = jnp.where(position == 0, -HW, offsets[:, 0])
    first_column = jnp.where(position == S_DEV - 1, HW, first_column)
    offsets = jnp.concatenate([first_column[:, None], offsets[:, 1:]], axis=1)
    return (position[:, None] + HW + offsets).astype(jnp.int32)


def set_ends(array, key, low, top_value):
    index_at = [jax.random.randint(jax.random.fold_in(key, axis), (), 0, length) for axis, length in enumerate(array.shape)]
    widest = array.shape.index(max(array.shape))
    neighbour = index_at[:widest] + [(index_at[widest] + 1) % array.shape[widest]] + index_at[widest + 1:]
    return array.at[tuple(index_at)].set(low).at[tuple(neighbour)].set(top_value)


def block_scale(stream_key, extent, pieces, least, top_value):
    level = 1.0
    for dim, parts in pieces:
        draws = jax.random.uniform(jax.random.fold_in(jax.random.fold_in(stream_key, 6), dim), (parts,), jnp.float32, least / len(pieces), top_value / len(pieces))
        level = level * jnp.repeat(jnp.exp(draws), extent[dim] // parts).reshape((-1,) + (1,) * (len(extent) - 1 - dim))
    return level


def routed_block(own_key, own, number, rows, amount, top, bound, skew):
    ranking = jax.random.permutation(own_key, amount)
    packed, common = shares(amount, rows * top, bound, skew, True), shares(amount, rows * top, bound, skew, False)
    places = jnp.arange(amount)

    def named(tallies, turn):
        used = int((tallies > 0).sum())
        fixed = max(1, used // 4)
        passed = fixed + (places - fixed + turn * (used - fixed)) % max(1, amount - fixed)
        return jnp.zeros((amount,), jnp.int32).at[ranking[jnp.where(places < fixed, places, passed)]].set(jnp.asarray(tallies, jnp.int32))

    tallies = jnp.where(number % 4 == 0, named(packed, number // 4), named(common, number - number // 4 - 1))
    mixed = jax.random.permutation(jax.random.fold_in(own, 3), amount)
    giver, taker = mixed[0:amount // 2 * 2:2], mixed[1:amount // 2 * 2:2]
    margin = jnp.minimum(tallies[giver] - 1, bound - tallies[taker]) // 2
    margin = jnp.where((giver == ranking[0]) | (taker == ranking[0]) | (tallies[taker] == 0), 0, jnp.maximum(margin, 0))
    passed = jax.random.randint(jax.random.fold_in(own, 4), (amount // 2,), 0, 1 << 20) % (margin + 1)
    tallies = tallies.at[giver].add(-passed).at[taker].add(passed)
    members = jnp.searchsorted(jnp.cumsum(tallies), jnp.arange(rows * top), side="right").astype(jnp.int32)
    table = members.reshape(top, rows).T
    table = table[jax.random.permutation(jax.random.fold_in(own, 1), rows)]
    turn = jax.random.randint(jax.random.fold_in(own, 2), (rows, 1), 0, top)
    return jnp.take_along_axis(table, (jnp.arange(top)[None, :] + turn) % top, axis=1)


def shares(number_of, total, limit, slope, full):
    weights = [(1 << 20) // math.isqrt(grade ** slope) + 1 for grade in range(1, number_of + 1)]
    largest = limit if full else min(limit, max(-(-total // number_of), total * weights[0] // sum(weights)))
    least = 1 if total - largest >= number_of - 1 else 0
    given, spare = [largest] + [least] * (number_of - 1), total - largest - least * (number_of - 1)
    while spare > 0:
        free = [i for i in range(1, number_of) if given[i] < largest] or [i for i in range(1, number_of) if given[i] < limit]
        mass, left = sum([weights[i] for i in free]), spare
        for i in free:
            addition = min(limit - given[i], max(1, left * weights[i] // mass), spare)
            given[i] = given[i] + addition
            spare = spare - addition
    return np.array(given)


def scatter_about(stream_key, shape, spread, limit, cuts=(), held_as=jnp.bfloat16):
    result = spread * jax.random.normal(stream_key, shape, jnp.float32)
    if cuts:
        result = result * block_scale(stream_key, shape, cuts, -0.22, 0.18)
    return jnp.clip(result, -limit, limit).astype(held_as)


def setup_inputs(seed: int = 0) -> dict:
    splits = jax.random.split(jax.random.key(seed), 9)
    field = scatter_about(splits[0], (SOURCES, COLS), 1.0, 6.0, ((0, 16), (1, 2)))
    grad_coef = scatter_about(splits[1], (2, K, SOURCES), 1.0, 6.0, ((2, 16),), jnp.float32)
    neighbours = draw_neighbours(jax.random.fold_in(splits[8], 71), 0)
    level_weight = jnp.clip(jnp.exp(jax.random.uniform(splits[3], (LEVELS,), jnp.float32, math.log(0.2), math.log(2.0))), 0.2, 2.0)
    src_index = set_ends(jax.random.randint(splits[4], (BLOCKS, SB), 0, S_DEV), jax.random.fold_in(splits[4], 1), 0, S_DEV - 1).astype(jnp.int32)
    tgt_index = set_ends(jax.random.randint(splits[5], (BLOCKS, TB), 0, T_DEV), jax.random.fold_in(splits[5], 1), 0, T_DEV - 1).astype(jnp.int32)
    block_dest_keys = jax.random.split(jax.random.fold_in(splits[6], 1), BLOCKS // B_DEV)
    block_dest_turns = jax.random.permutation(jax.random.fold_in(splits[6], 3), BLOCKS // B_DEV)
    block_dest = jax.vmap(lambda own, number: routed_block(jax.random.fold_in(splits[6], 2), own, number, B_DEV, N_SRC, 1, CAP, 2))(block_dest_keys, block_dest_turns).reshape((BLOCKS, 1))
    weights = scatter_about(splits[7], (BLOCKS, 3 * SB * TB), (12 * SB) ** -0.5, 0.21875, ((0, 16),))
    return {"field": field, "grad_coef": grad_coef, "neighbours": neighbours, "level_weight": level_weight, "src_index": src_index, "tgt_index": tgt_index, "block_dest": block_dest, "weights": weights}


def device_partial(extended, coefficients, neighbour_pos, source_cells, block_weights):
    own_values = extended[HW:HW + S_DEV]
    own_float = own_values.astype(jnp.float32)
    differ = extended[neighbour_pos].astype(jnp.float32) - own_float[:, None, :]
    grad_east = jnp.sum(coefficients[0].T[:, :, None] * differ, axis=1).astype(jnp.bfloat16)
    grad_north = jnp.sum(coefficients[1].T[:, :, None] * differ, axis=1).astype(jnp.bfloat16)
    recon = jnp.stack([own_values, grad_east, grad_north])
    picked = recon[:, source_cells]
    block_rows = jnp.transpose(picked, (1, 0, 2, 3)).reshape(source_cells.shape[0], 3 * SB, -1)
    shaped = block_weights.reshape(source_cells.shape[0], 3 * SB, TB)
    return jnp.einsum('bjt,bjc->btc', shaped.astype(jnp.float32), block_rows.astype(jnp.float32))


def reference(field, grad_coef, neighbours, level_weight, src_index, tgt_index, block_dest, weights):
    padded = jnp.concatenate([field[-HW:], field, field[:HW]], axis=0)
    coefficients = grad_coef.reshape(2, K, N_SRC, S_DEV).transpose(2, 0, 1, 3)
    neighbour_pos = neighbours.reshape(N_SRC, S_DEV, K)
    source_cells = src_index.reshape(N_SRC, B_DEV, SB)
    target_cells = ((block_dest[:, 0] * T_DEV)[:, None] + tgt_index).reshape(N_SRC, B_DEV * TB)
    block_weights = weights.reshape(N_SRC, B_DEV, 3 * SB * TB)

    def accumulate(total, inputs):
        device, coef_dev, nbr_dev, cells_dev, rows_dev, weights_dev = inputs
        extended = lax.dynamic_slice_in_dim(padded, device * S_DEV, S_DEV + 2 * HW, 0)
        partial_value = device_partial(extended, coef_dev, nbr_dev, cells_dev, weights_dev)
        return total.at[rows_dev].add(partial_value.reshape(-1, COLS)), None

    start = jnp.zeros((TARGETS, COLS), jnp.float32)
    devices = jnp.arange(N_SRC, dtype=jnp.int32)
    total, _ = lax.scan(accumulate, start, (devices, coefficients, neighbour_pos, source_cells, target_cells, block_weights))
    remapped = total.astype(jnp.bfloat16)
    column_total = jnp.einsum('tlf,l->ft', total.reshape(TARGETS, LEVELS, FIELDS), level_weight, precision=lax.Precision.HIGHEST)
    return remapped, column_total
```

```python
import functools

import jax
import jax.numpy as jnp
from jax import lax
from jax.experimental import pallas as pl
from jax.experimental.pallas import tpu as pltpu
from jax.sharding import PartitionSpec as P

FIELDS = 32
HW = 64
SB = 64
TB = 32
T_DEV = 1024
LANES = 128
SUB = 8
TILE = 128
GROUP = LANES // TB
GROUP_BITS = GROUP.bit_length() - 1
PIECE = 32
UNROLL = 4
BATCH = 16
SPAN = SB + SUB
PLANE = 4
PAIR = 2
BAND = 256
MESH = pl.DeviceIdType.MESH


def contract_first(a, b):
    return lax.dot_general(a, b, (((0,), (0,)), ((), ())), preferred_element_type=jnp.float32)


def contract_last(a, b):
    return lax.dot_general(a, b, (((1,), (1,)), ((), ())), preferred_element_type=jnp.float32)


def place(count):
    me = lax.axis_index("src")
    column = PLANE * PAIR
    return me // column, lax.rem(me // PLANE, PAIR), lax.rem(me, PLANE), count // column


def one_hot(mask):
    return jnp.where(mask, 1.0, 0.0).astype(jnp.bfloat16)


def plan(count, dest_ref, tgt_ref, src_ref, order_ref, start_ref, tags_ref, cells_ref):
    blocks = dest_ref.shape[1]
    outer, inner, plane, outers = place(count)
    steps = count // PLANE
    owner = dest_ref[...]
    turn = lax.shift_right_logical(owner, 3) - outer - 1
    turn = jnp.where(turn < 0, turn + outers, turn)
    same = jnp.bitwise_and(lax.shift_right_logical(owner, 2), 1) == inner
    step = 2 * turn + jnp.where(same, 1, 0)
    apart = jnp.bitwise_xor(jnp.bitwise_and(owner, PLANE - 1), plane)
    spot = jnp.where(apart == 3, 0, jnp.where(apart == 0, 3, apart))
    key = step * PLANE + spot
    slots = spot * steps + step

    keys = max(count, LANES)
    rows = lax.broadcasted_iota(jnp.int32, (keys, blocks), 0)
    hit = rows == key
    ones = one_hot(hit)
    before = one_hot(
        lax.broadcasted_iota(jnp.int32, (blocks, blocks), 0)
        < lax.broadcasted_iota(jnp.int32, (blocks, blocks), 1)
    )
    less = one_hot(
        lax.broadcasted_iota(jnp.int32, (keys, keys), 1)
        < lax.broadcasted_iota(jnp.int32, (keys, keys), 0)
    )
    prefix = jnp.dot(ones, before, preferred_element_type=jnp.float32)
    ahead = jnp.dot(less, ones, preferred_element_type=jnp.float32)
    starts = jnp.sum(ahead, axis=1, keepdims=True)
    rank = jnp.sum(jnp.where(hit, prefix, 0.0), axis=0, keepdims=True).astype(jnp.int32)
    at = rank + jnp.sum(jnp.where(hit, starts, 0.0), axis=0, keepdims=True).astype(jnp.int32)
    start_ref[...] = contract_last(
        jnp.ones((SUB, blocks), jnp.bfloat16), ahead.astype(jnp.bfloat16)
    ).astype(jnp.int32)
    here = one_hot(lax.broadcasted_iota(jnp.int32, (blocks, blocks), 0) == at)
    names = lax.broadcasted_iota(jnp.int32, (SUB, blocks), 1).astype(jnp.float32)
    order_ref[...] = contract_last(names.astype(jnp.bfloat16), here).astype(jnp.int32)
    source = src_ref[...]
    digits = [lax.shift_right_logical(source, 5), jnp.bitwise_and(source, 31)]
    moved = [contract_last(d.astype(jnp.float32).astype(jnp.bfloat16), here) for d in digits]
    cells_ref[...] = (moved[0] * 32.0 + moved[1]).astype(jnp.int32)

    line = slots * SUB + lax.shift_right_logical(rank, GROUP_BITS)
    lane = jnp.bitwise_and(rank, GROUP - 1)
    cell = tgt_ref[...] + 1
    high = lax.shift_right_logical(cell, 5).astype(jnp.float32)
    low = jnp.bitwise_and(cell, 31).astype(jnp.float32)
    found = [None, None]
    lines = lax.broadcasted_iota(jnp.int32, (count * SUB, blocks), 0) == line
    group = lax.broadcasted_iota(jnp.int32, (LANES, blocks), 0) // TB
    for q in range(GROUP):
        mine = one_hot(jnp.logical_and(lines, lane == q))
        for g, digit in enumerate((high, low)):
            spread = jnp.where(group == q, jnp.concatenate([digit] * GROUP, axis=0), 0.0)
            part = contract_last(mine, spread.astype(jnp.bfloat16))
            found[g] = part if found[g] is None else found[g] + part
    tags_ref[...] = (found[0] * 32.0 + found[1]).astype(jnp.int32) - 1


def prepare_kernel(
    count, field_ref, coef_ref, near_ref, dest_ref, tgt_ref, src_ref,
    recon, order_ref, start_ref, tags_ref, cells_ref,
    ext, mixes, out_sem, in_sem,
):
    cells = field_ref.shape[0]
    window = TILE + 2 * HW
    tiles = cells // TILE
    me = lax.axis_index("src")
    lev = lax.axis_index("lev")
    right = lax.rem(me + 1, count)
    left = lax.rem(me + count - 1, count)
    barrier = pltpu.get_barrier_semaphore()
    for other in (left, right):
        pl.semaphore_signal(barrier, inc=1, device_id=(other, lev), device_id_type=MESH)
    ext[HW:HW + cells, :] = field_ref[...]
    plan(count, dest_ref, tgt_ref, src_ref, order_ref, start_ref, tags_ref, cells_ref)

    def tile(t):
        base = pl.multiple_of(t * TILE, TILE)
        near = near_ref[:, pl.ds(base, TILE)] - base
        coef = [coef_ref[g, :, pl.ds(base, TILE)] for g in range(2)]
        totals = [-jnp.sum(coef[g], axis=0, keepdims=True) for g in range(2)]
        held = ext[pl.ds(base, window), :]
        rows = pl.multiple_of(base * SUB, TILE * SUB)
        recon[pl.ds(rows, TILE, stride=SUB), :] = field_ref[pl.ds(base, TILE), :].astype(
            jnp.float32
        )
        for w in range(0, window, PIECE):
            here = lax.broadcasted_iota(jnp.int32, (PIECE, TILE), 0) + w
            own = here == lax.broadcasted_iota(jnp.int32, (PIECE, TILE), 1) + HW
            mixed = [jnp.where(own, totals[g], 0.0) for g in range(2)]
            for k in range(near.shape[0]):
                hit = here == near[k:k + 1, :]
                for g in range(2):
                    mixed[g] = mixed[g] + jnp.where(hit, coef[g][k:k + 1, :], 0.0)
            for g in range(2):
                high = mixed[g].astype(jnp.bfloat16)
                rest = (mixed[g] - high.astype(jnp.float32)).astype(jnp.bfloat16)
                mixes[w:w + PIECE, 2 * g * TILE:(2 * g + 1) * TILE] = high
                mixes[w:w + PIECE, (2 * g + 1) * TILE:(2 * g + 2) * TILE] = rest
        for g in range(2):
            value = contract_first(mixes[:, 2 * g * TILE:(2 * g + 1) * TILE], held)
            value = value + contract_first(mixes[:, (2 * g + 1) * TILE:(2 * g + 2) * TILE], held)
            recon[pl.ds(rows + 1 + g, TILE, stride=SUB), :] = value

    @pl.loop(1, tiles // 2)
    def _(t):
        tile(t)

    pl.semaphore_wait(barrier, 2)
    low = pltpu.make_async_remote_copy(
        src_ref=field_ref.at[pl.ds(cells - HW, HW)], dst_ref=ext.at[pl.ds(0, HW)],
        send_sem=out_sem.at[0], recv_sem=in_sem.at[0],
        device_id=(right, lev), device_id_type=MESH,
    )
    high = pltpu.make_async_remote_copy(
        src_ref=field_ref.at[pl.ds(0, HW)], dst_ref=ext.at[pl.ds(HW + cells, HW)],
        send_sem=out_sem.at[1], recv_sem=in_sem.at[1],
        device_id=(left, lev), device_id_type=MESH,
    )
    low.start()
    high.start()

    @pl.loop(tiles // 2, tiles - 1)
    def _(t):
        tile(t)

    low.wait()
    high.wait()

    @pl.loop(0, 2)
    def _(e):
        tile(e * (tiles - 1))


def prepare(count, field, coef, near_t, dest_t, tgt_t, src_t):
    cells, columns = field.shape
    vmem = pl.BlockSpec(memory_space=pltpu.VMEM)
    return pl.pallas_call(
        functools.partial(prepare_kernel, count),
        out_shape=(
            jax.ShapeDtypeStruct((cells * SUB, columns), jnp.float32),
            jax.ShapeDtypeStruct((SUB, dest_t.shape[1]), jnp.int32),
            jax.ShapeDtypeStruct((SUB, max(count, LANES)), jnp.int32),
            jax.ShapeDtypeStruct((count * SUB, LANES), jnp.int32),
            jax.ShapeDtypeStruct(src_t.shape, jnp.int32),
        ),
        in_specs=[vmem] * 6,
        out_specs=(vmem,) * 5,
        scratch_shapes=[
            pltpu.VMEM((cells + 2 * HW, columns), jnp.bfloat16),
            pltpu.VMEM((TILE + 2 * HW, 4 * TILE), jnp.bfloat16),
            pltpu.SemaphoreType.DMA((2,)),
            pltpu.SemaphoreType.DMA((2,)),
        ],
        compiler_params=pltpu.CompilerParams(
            vmem_limit_bytes=24 << 20, collective_id=1, has_side_effects=True
        ),
        name="prepare",
    )(field, coef, near_t, dest_t, tgt_t, src_t)


def remap_kernel(
    count, capacity, level_count, lev_count,
    src_ref, order_ref, start_ref, level_ref, recon, weight_ref, tags_ref,
    remapped_ref, sum_ref,
    picked, compact, staged, land, seen, total, dense_out, dense_in, local_sum, other_sum,
    chunk_out, chunk_in, tag_out, tag_in, line_out, line_in, sum_sem,
):
    me = lax.axis_index("src")
    lev = lax.axis_index("lev")
    outer, inner, plane, outers = place(count)
    steps = count // PLANE
    base = me - plane
    rows = capacity * TB
    width = min(LANES, rows)
    lines = rows // width
    targets, columns = total.shape
    partner_lev = lax.rem(lev + 1, lev_count)
    peers = [
        base + PLANE - 1 - plane,
        base + plane + 1 - 2 * lax.rem(plane, 2),
        base + lax.rem(plane + 2, PLANE),
    ]
    partner = me + PLANE * (1 - 2 * inner)

    def mirror(turn):
        return lax.rem(outer + turn, outers) * PLANE * PAIR + inner * PLANE + plane

    barrier = pltpu.get_barrier_semaphore()
    for other in peers + [partner]:
        pl.semaphore_signal(barrier, inc=1, device_id=(other, lev), device_id_type=MESH)

    @pl.loop(1, outers)
    def _(t):
        pl.semaphore_signal(barrier, inc=1, device_id=(mirror(t), lev), device_id_type=MESH)

    pl.semaphore_signal(barrier, inc=1, device_id=(me, partner_lev), device_id_type=MESH)

    @pl.loop(0, compact.shape[0] // SUB)
    def _(n):
        compact[pl.ds(n * SUB, SUB)] = jnp.zeros((SUB, TB, columns), jnp.bfloat16)

    seen[PLANE - 1] = tags_ref[PLANE - 1]
    pl.semaphore_wait(barrier, PLANE + outers)

    def tag_copy(spot):
        return pltpu.make_async_remote_copy(
            src_ref=tags_ref.at[spot], dst_ref=seen.at[spot],
            send_sem=tag_out.at[spot], recv_sem=tag_in.at[spot],
            device_id=(peers[spot], lev), device_id_type=MESH,
        )

    def chunk_copy(step, spot):
        return pltpu.make_async_remote_copy(
            src_ref=staged.at[step, spot], dst_ref=land.at[step, spot],
            send_sem=chunk_out.at[step, spot], recv_sem=chunk_in.at[step, spot],
            device_id=(peers[spot], lev), device_id_type=MESH,
        )

    def line_copy(step, to):
        return pltpu.make_async_remote_copy(
            src_ref=dense_out.at[step], dst_ref=dense_in.at[step],
            send_sem=line_out.at[step], recv_sem=line_in.at[step],
            device_id=(to, lev), device_id_type=MESH,
        )

    for spot in range(PLANE - 1):
        tag_copy(spot).start()

    def one(i, buffer):
        for begin in range(0, SB, BATCH):
            found = [recon[src_ref[begin + j, i]] for j in range(BATCH)]
            for j in range(BATCH):
                to = ((begin + j) % GROUP) * (SB // GROUP) + (begin + j) // GROUP
                buffer[pl.ds(to, 3, stride=SPAN), :] = found[j][0:3, :]
        held = weight_ref[order_ref[0, i]]
        whole = None
        for q in range(GROUP):
            parts = [
                buffer[pl.ds(c * SPAN + q * (SB // GROUP), SB // GROUP), :] for c in range(3)
            ]
            terms = jnp.concatenate(parts, axis=0).astype(jnp.bfloat16)
            product = contract_first(held[:, q * TB:(q + 1) * TB], terms)
            whole = product if whole is None else whole + product
        compact[i] = whole.astype(jnp.bfloat16)

    def stage(step, spot):
        chunk = compact[pl.ds(start_ref[0, step * PLANE + spot], capacity)].reshape(rows, columns)
        if spot < PLANE - 1:
            staged[step, spot] = chunk
            chunk_copy(step, spot).start()
        else:
            land[step, spot] = chunk

    unroll = min(UNROLL, capacity)

    @pl.loop(0, steps // 2)
    def _(step):
        for spot in range(PLANE):

            @pl.loop(0, capacity // unroll)
            def _(n, spot=spot):
                first = (step * PLANE + spot) * capacity + n * unroll
                for m in range(unroll):
                    one(first + m, picked.at[m])

            stage(step, spot)

    @pl.loop(steps // 2, steps)
    def _(step):
        for spot in range(PLANE):
            stage(step, spot)

    for spot in range(PLANE - 1):
        tag_copy(spot).wait_recv()

    def add(step, spot, fresh):
        cell = seen[spot, step]
        part = lax.shift_right_arithmetic(cell, 8)
        low = jnp.bitwise_and(cell, BAND - 1)
        chunk = land[step, spot]
        where = lax.broadcasted_iota(jnp.int32, (BAND, width), 0).astype(jnp.float32)
        where = where.astype(jnp.bfloat16)
        for h in range(targets // BAND):
            mark = jnp.where(part == h, low, -1).astype(jnp.float32).astype(jnp.bfloat16)
            hits = [
                jnp.where(where == mark[m:m + 1, :width], 1.0, 0.0).astype(jnp.bfloat16)
                for m in range(lines)
            ]
            hits = hits[0] if lines == 1 else jnp.concatenate(hits, axis=1)
            sums = jnp.dot(hits, chunk, preferred_element_type=jnp.float32)
            band = pl.ds(h * BAND, BAND)
            total[band, :] = sums if fresh else total[band, :] + sums

    def gather(step):
        add(step, PLANE - 1, True)
        for spot in range(PLANE - 1):

            def ready(spot=spot):
                chunk_copy(step, spot).wait_recv()

            ready()
            add(step, spot, False)

    def near(step):
        gather(step)
        dense_out[step] = total[...].astype(jnp.bfloat16)
        line_copy(step, partner).start()

    @pl.loop(0, outers - 1)
    def _(turn):
        step = 2 * turn
        near(step)
        gather(step + 1)
        line_copy(step, partner).wait_recv()
        both = total[...] + dense_in[step].astype(jnp.float32)
        dense_out[step + 1] = both.astype(jnp.bfloat16)
        line_copy(step + 1, mirror(turn + 1)).start()

    near(steps - 2)
    gather(steps - 1)
    line_copy(steps - 2, partner).wait_recv()
    total[...] += dense_in[steps - 2].astype(jnp.float32)

    @pl.loop(0, outers - 1)
    def _(turn):
        line_copy(2 * turn + 1, mirror(turn + 1)).wait_recv()
        total[...] += dense_in[2 * turn + 1].astype(jnp.float32)

    result = total[...]
    remapped_ref[...] = result.astype(jnp.bfloat16)
    start = lev * level_count
    which = lax.broadcasted_iota(jnp.int32, (FIELDS, columns), 1)
    line = lax.broadcasted_iota(jnp.int32, (FIELDS, columns), 0)
    mix = jnp.zeros((FIELDS, columns), jnp.float32)
    for l in range(level_count):
        mix = jnp.where(which == line + l * FIELDS, level_ref[start + l], mix)
    local_sum[...] = lax.dot_general(
        mix,
        result,
        (((1,), (1,)), ((), ())),
        precision=lax.Precision.HIGHEST,
        preferred_element_type=jnp.float32,
    )
    swap = pltpu.make_async_remote_copy(
        src_ref=local_sum, dst_ref=other_sum, send_sem=sum_sem.at[0], recv_sem=sum_sem.at[1],
        device_id=(me, partner_lev), device_id_type=MESH,
    )
    swap.start()
    for spot in range(PLANE - 1):
        tag_copy(spot).wait_send()

    @pl.loop(0, steps)
    def _(step):
        for spot in range(PLANE - 1):
            chunk_copy(step, spot).wait_send()

    @pl.loop(0, steps - 1)
    def _(step):
        line_copy(step, partner).wait_send()

    swap.wait()
    sum_ref[...] = local_sum[...] + other_sum[...]


def remap(count, capacity, lev_count, level_count, src_t, order, start, level, recon, weight, tags):
    columns = recon.shape[2]
    blocks = src_t.shape[1]
    steps = count // PLANE
    rows = capacity * TB
    smem = pl.BlockSpec(memory_space=pltpu.SMEM)
    vmem = pl.BlockSpec(memory_space=pltpu.VMEM)
    dma = pltpu.SemaphoreType.DMA
    chunk = (rows, columns)
    dense = (T_DEV, columns)
    return pl.pallas_call(
        functools.partial(remap_kernel, count, capacity, level_count, lev_count),
        out_shape=(
            jax.ShapeDtypeStruct(dense, jnp.bfloat16),
            jax.ShapeDtypeStruct((FIELDS, T_DEV), jnp.float32),
        ),
        in_specs=[smem] * 4 + [vmem] * 3,
        out_specs=(vmem, vmem),
        scratch_shapes=[
            pltpu.VMEM((UNROLL, 3 * SPAN, columns), jnp.float32),
            pltpu.VMEM((-(-(blocks + capacity) // SUB) * SUB, TB, columns), jnp.bfloat16),
            pltpu.VMEM((steps, PLANE - 1) + chunk, jnp.bfloat16),
            pltpu.VMEM((steps, PLANE) + chunk, jnp.bfloat16),
            pltpu.VMEM((PLANE, steps, SUB, LANES), jnp.int32),
            pltpu.VMEM(dense, jnp.float32),
            pltpu.VMEM((steps - 1,) + dense, jnp.bfloat16),
            pltpu.VMEM((steps - 1,) + dense, jnp.bfloat16),
            pltpu.VMEM((FIELDS, T_DEV), jnp.float32),
            pltpu.VMEM((FIELDS, T_DEV), jnp.float32),
            dma((steps, PLANE - 1)),
            dma((steps, PLANE - 1)),
            dma((PLANE - 1,)),
            dma((PLANE - 1,)),
            dma((steps - 1,)),
            dma((steps - 1,)),
            dma((2,)),
        ],
        compiler_params=pltpu.CompilerParams(
            vmem_limit_bytes=52 << 20, collective_id=0, has_side_effects=True
        ),
        name="remap",
    )(src_t, order, start, level, recon, weight, tags)


def shards(field, grad_coef, neighbours, level_weight, src_index, tgt_index, block_dest, weights):
    count = lax.axis_size("src")
    columns = field.shape[1]
    blocks = src_index.shape[0]
    capacity = 2 * blocks // count
    steps = count // PLANE
    shaped = weights.reshape(blocks, 3 * SB * TB // LANES, LANES)
    recon, order, start, tags, cells = prepare(
        count, field, grad_coef, neighbours.T, block_dest.T, tgt_index.T, src_index.T
    )
    return remap(
        count, capacity, lax.axis_size("lev"), columns // FIELDS, cells, order, start,
        level_weight, recon.reshape(-1, SUB, columns), shaped, tags.reshape(PLANE, steps, SUB, LANES),
    )


def solution(mesh):
    placed = (
        P("src", "lev"),
        P(None, None, "src"),
        P("src", None),
        P(),
        P("src", None),
        P("src", None),
        P("src", None),
        P("src", None),
    )
    return jax.shard_map(
        shards,
        mesh=mesh,
        in_specs=placed,
        out_specs=(P("src", "lev"), P(None, "src")),
        check_vma=False,
    )
```

```python
import functools

import jax
import jax.numpy as jnp
from jax import lax
from jax.experimental import pallas as pl
from jax.experimental.pallas import tpu as pltpu
from jax.sharding import PartitionSpec as P

FIELDS = 32
HW = 64
SB = 64
TB = 32
T_DEV = 1024
LANES = 128
SUB = 8
TILE = 128
GROUP = LANES // TB
GROUP_BITS = GROUP.bit_length() - 1
PIECE = 32
UNROLL = 4
BATCH = 16
SPAN = SB + SUB
PLANE = 4
PAIR = 2
BAND = 256
MESH = pl.DeviceIdType.MESH


def contract_first(a, b):
    return lax.dot_general(a, b, (((0,), (0,)), ((), ())), preferred_element_type=jnp.float32)


def contract_last(a, b):
    return lax.dot_general(a, b, (((1,), (1,)), ((), ())), preferred_element_type=jnp.float32)


def place(count):
    me = lax.axis_index("src")
    column = PLANE * PAIR
    return me // column, lax.rem(me // PLANE, PAIR), lax.rem(me, PLANE), count // column


def one_hot(mask):
    return jnp.where(mask, jnp.bfloat16(1), jnp.bfloat16(0))


def plan(count, dest_ref, tgt_ref, src_ref, order_ref, start_ref, tags_ref, cells_ref):
    blocks = dest_ref.shape[1]
    outer, inner, plane, outers = place(count)
    steps = count // PLANE
    owner = dest_ref[...]
    turn = lax.shift_right_logical(owner, 3) - outer - 1
    turn = jnp.where(turn < 0, turn + outers, turn)
    same = jnp.bitwise_and(lax.shift_right_logical(owner, 2), 1) == inner
    step = 2 * turn + jnp.where(same, 1, 0)
    apart = jnp.bitwise_xor(jnp.bitwise_and(owner, PLANE - 1), plane)
    spot = jnp.where(apart == 3, 0, jnp.where(apart == 0, 3, apart))
    key = step * PLANE + spot
    slots = spot * steps + step

    keys = max(count, LANES)
    rows = lax.broadcasted_iota(jnp.int32, (keys, blocks), 0)
    hit = rows == key
    ones = one_hot(hit)
    before = one_hot(
        lax.broadcasted_iota(jnp.int32, (blocks, blocks), 0)
        < lax.broadcasted_iota(jnp.int32, (blocks, blocks), 1)
    )
    less = one_hot(
        lax.broadcasted_iota(jnp.int32, (keys, keys), 1)
        < lax.broadcasted_iota(jnp.int32, (keys, keys), 0)
    )
    prefix = jnp.dot(ones, before, preferred_element_type=jnp.float32)
    ahead = jnp.dot(less, ones, preferred_element_type=jnp.float32)
    starts = jnp.sum(ahead, axis=1, keepdims=True)
    rank = jnp.sum(jnp.where(hit, prefix, 0.0), axis=0, keepdims=True).astype(jnp.int32)
    at = rank + jnp.sum(jnp.where(hit, starts, 0.0), axis=0, keepdims=True).astype(jnp.int32)
    start_ref[...] = contract_last(
        jnp.ones((SUB, blocks), jnp.bfloat16), ahead.astype(jnp.bfloat16)
    ).astype(jnp.int32)
    here = one_hot(lax.broadcasted_iota(jnp.int32, (blocks, blocks), 0) == at)
    names = lax.broadcasted_iota(jnp.int32, (SUB, blocks), 1).astype(jnp.float32)
    order_ref[...] = contract_last(names.astype(jnp.bfloat16), here).astype(jnp.int32)
    source = src_ref[...]
    digits = [lax.shift_right_logical(source, 5), jnp.bitwise_and(source, 31)]
    moved = [contract_last(here, d.astype(jnp.float32).astype(jnp.bfloat16)) for d in digits]
    cells_ref[...] = (moved[0] * 32.0 + moved[1]).astype(jnp.int32)

    line = slots * SUB + lax.shift_right_logical(rank, GROUP_BITS)
    lane = jnp.bitwise_and(rank, GROUP - 1)
    cell = tgt_ref[...] + 1
    high = lax.shift_right_logical(cell, 5).astype(jnp.float32)
    low = jnp.bitwise_and(cell, 31).astype(jnp.float32)
    found = [None, None]
    lines = lax.broadcasted_iota(jnp.int32, (count * SUB, blocks), 0) == line
    group = lax.broadcasted_iota(jnp.int32, (LANES, blocks), 0) // TB
    for q in range(GROUP):
        mine = one_hot(jnp.logical_and(lines, lane == q))
        for g, digit in enumerate((high, low)):
            spread = jnp.where(group == q, jnp.concatenate([digit] * GROUP, axis=0), 0.0)
            part = contract_last(mine, spread.astype(jnp.bfloat16))
            found[g] = part if found[g] is None else found[g] + part
    tags_ref[...] = (found[0] * 32.0 + found[1]).astype(jnp.int32) - 1


def prepare_kernel(
    count, field_ref, coef_ref, near_ref, dest_ref, tgt_ref, src_ref,
    recon, order_ref, start_ref, tags_ref, cells_ref,
    ext, mixes, out_sem, in_sem,
):
    cells = field_ref.shape[0]
    window = TILE + 2 * HW
    tiles = cells // TILE
    me = lax.axis_index("src")
    lev = lax.axis_index("lev")
    right = lax.rem(me + 1, count)
    left = lax.rem(me + count - 1, count)
    barrier = pltpu.get_barrier_semaphore()
    for other in (left, right):
        pl.semaphore_signal(barrier, inc=1, device_id=(other, lev), device_id_type=MESH)
    ext[HW:HW + cells, :] = field_ref[...]
    plan(count, dest_ref, tgt_ref, src_ref, order_ref, start_ref, tags_ref, cells_ref)

    def tile(t):
        base = pl.multiple_of(t * TILE, TILE)
        near = near_ref[:, pl.ds(base, TILE)] - base
        coef = [coef_ref[g, :, pl.ds(base, TILE)] for g in range(2)]
        totals = [-jnp.sum(coef[g], axis=0, keepdims=True) for g in range(2)]
        held = ext[pl.ds(base, window), :]
        rows = pl.multiple_of(base * SUB, TILE * SUB)
        recon[pl.ds(rows, TILE, stride=SUB), :] = field_ref[pl.ds(base, TILE), :].astype(
            jnp.float32
        )
        for w in range(0, window, PIECE):
            here = lax.broadcasted_iota(jnp.int32, (PIECE, TILE), 0) + w
            own = here == lax.broadcasted_iota(jnp.int32, (PIECE, TILE), 1) + HW
            mixed = [jnp.where(own, totals[g], 0.0) for g in range(2)]
            for k in range(near.shape[0]):
                hit = here == near[k:k + 1, :]
                for g in range(2):
                    mixed[g] = mixed[g] + jnp.where(hit, coef[g][k:k + 1, :], 0.0)
            for g in range(2):
                high = mixed[g].astype(jnp.bfloat16)
                rest = (mixed[g] - high.astype(jnp.float32)).astype(jnp.bfloat16)
                mixes[w:w + PIECE, 2 * g * TILE:(2 * g + 1) * TILE] = high
                mixes[w:w + PIECE, (2 * g + 1) * TILE:(2 * g + 2) * TILE] = rest
        for g in range(2):
            value = contract_first(mixes[:, 2 * g * TILE:(2 * g + 1) * TILE], held)
            value = value + contract_first(mixes[:, (2 * g + 1) * TILE:(2 * g + 2) * TILE], held)
            recon[pl.ds(rows + 1 + g, TILE, stride=SUB), :] = value

    @pl.loop(1, tiles // 2)
    def _(t):
        tile(t)

    pl.semaphore_wait(barrier, 2)
    low = pltpu.make_async_remote_copy(
        src_ref=field_ref.at[pl.ds(cells - HW, HW)], dst_ref=ext.at[pl.ds(0, HW)],
        send_sem=out_sem.at[0], recv_sem=in_sem.at[0],
        device_id=(right, lev), device_id_type=MESH,
    )
    high = pltpu.make_async_remote_copy(
        src_ref=field_ref.at[pl.ds(0, HW)], dst_ref=ext.at[pl.ds(HW + cells, HW)],
        send_sem=out_sem.at[1], recv_sem=in_sem.at[1],
        device_id=(left, lev), device_id_type=MESH,
    )
    low.start()
    high.start()

    @pl.loop(tiles // 2, tiles - 1)
    def _(t):
        tile(t)

    low.wait()
    high.wait()

    @pl.loop(0, 2)
    def _(e):
        tile(e * (tiles - 1))


def prepare(count, field, coef, near_t, dest_t, tgt_t, src_t):
    cells, columns = field.shape
    vmem = pl.BlockSpec(memory_space=pltpu.VMEM)
    return pl.pallas_call(
        functools.partial(prepare_kernel, count),
        out_shape=(
            jax.ShapeDtypeStruct((cells * SUB, columns), jnp.float32),
            jax.ShapeDtypeStruct((SUB, dest_t.shape[1]), jnp.int32),
            jax.ShapeDtypeStruct((SUB, max(count, LANES)), jnp.int32),
            jax.ShapeDtypeStruct((count * SUB, LANES), jnp.int32),
            jax.ShapeDtypeStruct(src_t.shape[::-1], jnp.int32),
        ),
        in_specs=[vmem] * 6,
        out_specs=(vmem,) * 5,
        scratch_shapes=[
            pltpu.VMEM((cells + 2 * HW, columns), jnp.bfloat16),
            pltpu.VMEM((TILE + 2 * HW, 4 * TILE), jnp.bfloat16),
            pltpu.SemaphoreType.DMA((2,)),
            pltpu.SemaphoreType.DMA((2,)),
        ],
        compiler_params=pltpu.CompilerParams(
            vmem_limit_bytes=24 << 20, collective_id=1, has_side_effects=True
        ),
        name="prepare",
    )(field, coef, near_t, dest_t, tgt_t, src_t)


def remap_kernel(
    count, capacity, level_count, lev_count,
    src_ref, order_ref, start_ref, level_ref, recon, weight_ref, tags_ref,
    remapped_ref, sum_ref,
    picked, compact, staged, land, seen, total, dense_out, dense_in, local_sum, other_sum,
    chunk_out, chunk_in, tag_out, tag_in, line_out, line_in, sum_sem,
):
    me = lax.axis_index("src")
    lev = lax.axis_index("lev")
    outer, inner, plane, outers = place(count)
    steps = count // PLANE
    base = me - plane
    rows = capacity * TB
    width = min(LANES, rows)
    lines = rows // width
    targets, columns = total.shape
    partner_lev = lax.rem(lev + 1, lev_count)
    peers = [
        base + PLANE - 1 - plane,
        base + plane + 1 - 2 * lax.rem(plane, 2),
        base + lax.rem(plane + 2, PLANE),
    ]
    partner = me + PLANE * (1 - 2 * inner)

    def mirror(turn):
        return lax.rem(outer + turn, outers) * PLANE * PAIR + inner * PLANE + plane

    barrier = pltpu.get_barrier_semaphore()
    for other in peers + [partner]:
        pl.semaphore_signal(barrier, inc=1, device_id=(other, lev), device_id_type=MESH)

    @pl.loop(1, outers)
    def _(t):
        pl.semaphore_signal(barrier, inc=1, device_id=(mirror(t), lev), device_id_type=MESH)

    pl.semaphore_signal(barrier, inc=1, device_id=(me, partner_lev), device_id_type=MESH)

    @pl.loop(0, compact.shape[0] // SUB)
    def _(n):
        compact[pl.ds(n * SUB, SUB)] = jnp.zeros((SUB, TB, columns), jnp.bfloat16)

    seen[PLANE - 1] = tags_ref[PLANE - 1]
    pl.semaphore_wait(barrier, PLANE + outers)

    def tag_copy(spot):
        return pltpu.make_async_remote_copy(
            src_ref=tags_ref.at[spot], dst_ref=seen.at[spot],
            send_sem=tag_out.at[spot], recv_sem=tag_in.at[spot],
            device_id=(peers[spot], lev), device_id_type=MESH,
        )

    def chunk_copy(step, spot):
        return pltpu.make_async_remote_copy(
            src_ref=staged.at[step, spot], dst_ref=land.at[step, spot],
            send_sem=chunk_out.at[step, spot], recv_sem=chunk_in.at[step, spot],
            device_id=(peers[spot], lev), device_id_type=MESH,
        )

    def line_copy(step, to):
        return pltpu.make_async_remote_copy(
            src_ref=dense_out.at[step], dst_ref=dense_in.at[step],
            send_sem=line_out.at[step], recv_sem=line_in.at[step],
            device_id=(to, lev), device_id_type=MESH,
        )

    for spot in range(PLANE - 1):
        tag_copy(spot).start()

    def fetch(first, unroll):
        for begin in range(0, SB, BATCH):
            for m in range(unroll):
                index = src_ref.at[first + m]
                buffer = picked.at[m]
                found = [recon[index[begin + j]] for j in range(BATCH)]
                for j in range(BATCH):
                    to = ((begin + j) % GROUP) * (SB // GROUP) + (begin + j) // GROUP
                    buffer[pl.ds(to, 3, stride=SPAN), :] = found[j][0:3, :]

    def one(i, buffer):
        held = weight_ref[order_ref[0, i]]
        whole = None
        for q in range(GROUP):
            parts = [
                buffer[pl.ds(c * SPAN + q * (SB // GROUP), SB // GROUP), :] for c in range(3)
            ]
            terms = jnp.concatenate(parts, axis=0).astype(jnp.bfloat16)
            product = contract_first(held[:, q * TB:(q + 1) * TB], terms)
            whole = product if whole is None else whole + product
        compact[i] = whole.astype(jnp.bfloat16)

    def stage(step, spot):
        chunk = compact[pl.ds(start_ref[0, step * PLANE + spot], capacity)].reshape(rows, columns)
        if spot < PLANE - 1:
            staged[step, spot] = chunk
            chunk_copy(step, spot).start()
        else:
            land[step, spot] = chunk

    unroll = min(UNROLL, capacity)

    @pl.loop(0, steps // 2)
    def _(step):
        for spot in range(PLANE):

            @pl.loop(0, capacity // unroll)
            def _(n, spot=spot):
                first = (step * PLANE + spot) * capacity + n * unroll
                fetch(first, unroll)
                for m in range(unroll):
                    one(first + m, picked.at[m])

            stage(step, spot)

    @pl.loop(steps // 2, steps)
    def _(step):
        for spot in range(PLANE):
            stage(step, spot)

    for spot in range(PLANE - 1):
        tag_copy(spot).wait_recv()

    def add(step, spot, fresh):
        cell = seen[spot, step]
        part = lax.shift_right_arithmetic(cell, 8)
        low = jnp.bitwise_and(cell, BAND - 1)
        chunk = land[step, spot]
        where = lax.broadcasted_iota(jnp.int32, (BAND, width), 0).astype(jnp.float32)
        where = where.astype(jnp.bfloat16)
        for h in range(targets // BAND):
            mark = jnp.where(part == h, low, -1).astype(jnp.float32).astype(jnp.bfloat16)
            hits = [
                one_hot(where == mark[m:m + 1, :width]) for m in range(lines)
            ]
            hits = hits[0] if lines == 1 else jnp.concatenate(hits, axis=1)
            sums = jnp.dot(hits, chunk, preferred_element_type=jnp.float32)
            band = pl.ds(h * BAND, BAND)
            total[band, :] = sums if fresh else total[band, :] + sums

    def gather(step):
        add(step, PLANE - 1, True)
        for spot in range(PLANE - 1):

            def ready(spot=spot):
                chunk_copy(step, spot).wait_recv()

            ready()
            add(step, spot, False)

    def near(step):
        gather(step)
        dense_out[step] = total[...].astype(jnp.bfloat16)
        line_copy(step, partner).start()

    @pl.loop(0, outers - 1)
    def _(turn):
        step = 2 * turn
        near(step)
        gather(step + 1)
        line_copy(step, partner).wait_recv()
        both = total[...] + dense_in[step].astype(jnp.float32)
        dense_out[step + 1] = both.astype(jnp.bfloat16)
        line_copy(step + 1, mirror(turn + 1)).start()

    near(steps - 2)
    gather(steps - 1)
    line_copy(steps - 2, partner).wait_recv()
    total[...] += dense_in[steps - 2].astype(jnp.float32)

    @pl.loop(0, outers - 1)
    def _(turn):
        line_copy(2 * turn + 1, mirror(turn + 1)).wait_recv()
        total[...] += dense_in[2 * turn + 1].astype(jnp.float32)

    result = total[...]
    remapped_ref[...] = result.astype(jnp.bfloat16)
    start = lev * level_count
    which = lax.broadcasted_iota(jnp.int32, (FIELDS, columns), 1)
    line = lax.broadcasted_iota(jnp.int32, (FIELDS, columns), 0)
    mix = jnp.zeros((FIELDS, columns), jnp.float32)
    for l in range(level_count):
        mix = jnp.where(which == line + l * FIELDS, level_ref[start + l], mix)
    local_sum[...] = lax.dot_general(
        mix,
        result,
        (((1,), (1,)), ((), ())),
        precision=lax.Precision.HIGHEST,
        preferred_element_type=jnp.float32,
    )
    swap = pltpu.make_async_remote_copy(
        src_ref=local_sum, dst_ref=other_sum, send_sem=sum_sem.at[0], recv_sem=sum_sem.at[1],
        device_id=(me, partner_lev), device_id_type=MESH,
    )
    swap.start()
    for spot in range(PLANE - 1):
        tag_copy(spot).wait_send()

    @pl.loop(0, steps)
    def _(step):
        for spot in range(PLANE - 1):
            chunk_copy(step, spot).wait_send()

    @pl.loop(0, steps - 1)
    def _(step):
        line_copy(step, partner).wait_send()

    swap.wait()
    sum_ref[...] = local_sum[...] + other_sum[...]


def remap(count, capacity, lev_count, level_count, cells, order, start, level, recon, weight, tags):
    columns = recon.shape[2]
    blocks = cells.shape[0]
    steps = count // PLANE
    rows = capacity * TB
    smem = pl.BlockSpec(memory_space=pltpu.SMEM)
    vmem = pl.BlockSpec(memory_space=pltpu.VMEM)
    dma = pltpu.SemaphoreType.DMA
    chunk = (rows, columns)
    dense = (T_DEV, columns)
    return pl.pallas_call(
        functools.partial(remap_kernel, count, capacity, level_count, lev_count),
        out_shape=(
            jax.ShapeDtypeStruct(dense, jnp.bfloat16),
            jax.ShapeDtypeStruct((FIELDS, T_DEV), jnp.float32),
        ),
        in_specs=[smem] * 4 + [vmem] * 3,
        out_specs=(vmem, vmem),
        scratch_shapes=[
            pltpu.VMEM((UNROLL, 3 * SPAN, columns), jnp.float32),
            pltpu.VMEM((-(-(blocks + capacity) // SUB) * SUB, TB, columns), jnp.bfloat16),
            pltpu.VMEM((steps, PLANE - 1) + chunk, jnp.bfloat16),
            pltpu.VMEM((steps, PLANE) + chunk, jnp.bfloat16),
            pltpu.VMEM((PLANE, steps, SUB, LANES), jnp.int32),
            pltpu.VMEM(dense, jnp.float32),
            pltpu.VMEM((steps - 1,) + dense, jnp.bfloat16),
            pltpu.VMEM((steps - 1,) + dense, jnp.bfloat16),
            pltpu.VMEM((FIELDS, T_DEV), jnp.float32),
            pltpu.VMEM((FIELDS, T_DEV), jnp.float32),
            dma((steps, PLANE - 1)),
            dma((steps, PLANE - 1)),
            dma((PLANE - 1,)),
            dma((PLANE - 1,)),
            dma((steps - 1,)),
            dma((steps - 1,)),
            dma((2,)),
        ],
        compiler_params=pltpu.CompilerParams(
            vmem_limit_bytes=(12 << 20) + steps * (3 << 18), collective_id=0, has_side_effects=True
        ),
        name="remap",
    )(cells, order, start, level, recon, weight, tags)


def shards(field, grad_coef, neighbours, level_weight, src_index, tgt_index, block_dest, weights):
    count = lax.axis_size("src")
    columns = field.shape[1]
    blocks = src_index.shape[0]
    capacity = 2 * blocks // count
    steps = count // PLANE
    shaped = weights.reshape(blocks, 3 * SB * TB // LANES, LANES)
    recon, order, start, tags, cells = prepare(
        count, field, grad_coef, neighbours.T, block_dest.T, tgt_index.T, src_index.T
    )
    return remap(
        count, capacity, lax.axis_size("lev"), columns // FIELDS, cells, order, start,
        level_weight, recon.reshape(-1, SUB, columns), shaped, tags.reshape(PLANE, steps, SUB, LANES),
    )


def solution(mesh):
    placed = (
        P("src", "lev"),
        P(None, None, "src"),
        P("src", None),
        P(),
        P("src", None),
        P("src", None),
        P("src", None),
        P("src", None),
    )
    return jax.shard_map(
        shards,
        mesh=mesh,
        in_specs=placed,
        out_specs=(P("src", "lev"), P(None, "src")),
        check_vma=False,
    )
```

```python
import functools

import jax
import jax.numpy as jnp
from jax import lax
from jax.experimental import pallas as pl
from jax.experimental.pallas import tpu as pltpu
from jax.sharding import PartitionSpec as P

FIELDS = 32
HW = 64
SB = 64
TB = 32
T_DEV = 1024
LANES = 128
SUB = 8
TILE = 128
GROUP = LANES // TB
GROUP_BITS = GROUP.bit_length() - 1
PIECE = 32
UNROLL = 4
BATCH = 16
SPAN = SB + SUB
PLANE = 4
PAIR = 2
BAND = 256
MESH = pl.DeviceIdType.MESH


def contract_first(a, b):
    return lax.dot_general(a, b, (((0,), (0,)), ((), ())), preferred_element_type=jnp.float32)


def contract_last(a, b):
    return lax.dot_general(a, b, (((1,), (1,)), ((), ())), preferred_element_type=jnp.float32)


def place(count):
    me = lax.axis_index("src")
    column = PLANE * PAIR
    return me // column, lax.rem(me // PLANE, PAIR), lax.rem(me, PLANE), count // column


def one_hot(mask):
    return jnp.where(mask, jnp.bfloat16(1), jnp.bfloat16(0))


def plan(count, lines, dest_ref, tgt_ref, src_ref, order_ref, start_ref, tags_ref, cells_ref):
    lev = lax.axis_index("lev")
    blocks = dest_ref.shape[1]
    outer, inner, plane, outers = place(count)
    steps = count // PLANE
    owner = dest_ref[...]
    turn = lax.shift_right_logical(owner, 3) - outer - 1
    turn = jnp.where(turn < 0, turn + outers, turn)
    same = jnp.bitwise_and(lax.shift_right_logical(owner, 2), 1) == inner
    step = 2 * turn + jnp.where(same, 1, 0)
    apart = jnp.bitwise_xor(jnp.bitwise_and(owner, PLANE - 1), plane)
    spot = jnp.where(apart == 3, 0, jnp.where(apart == 0, 3, apart))
    key = step * PLANE + spot
    slots = spot * steps + step

    keys = max(count, LANES)
    rows = lax.broadcasted_iota(jnp.int32, (keys, blocks), 0)
    hit = rows == key
    ones = one_hot(hit)
    before = one_hot(
        lax.broadcasted_iota(jnp.int32, (blocks, blocks), 0)
        < lax.broadcasted_iota(jnp.int32, (blocks, blocks), 1)
    )
    less = one_hot(
        lax.broadcasted_iota(jnp.int32, (keys, keys), 1)
        < lax.broadcasted_iota(jnp.int32, (keys, keys), 0)
    )
    prefix = jnp.dot(ones, before, preferred_element_type=jnp.float32)
    ahead = jnp.dot(less, ones, preferred_element_type=jnp.float32)
    starts = jnp.sum(ahead, axis=1, keepdims=True)
    rank = jnp.sum(jnp.where(hit, prefix, 0.0), axis=0, keepdims=True).astype(jnp.int32)
    first = jnp.sum(jnp.where(hit, starts, 0.0), axis=0, keepdims=True).astype(jnp.int32)
    at = rank + first
    core = jnp.bitwise_and(at, 1)
    turn_at = lax.shift_right_logical(at, 1) - lax.shift_right_logical(first + 1 - core, 1)
    every = contract_last(jnp.ones((SUB, blocks), jnp.bfloat16), ahead.astype(jnp.bfloat16))
    start_ref[...] = lax.shift_right_logical(every.astype(jnp.int32) + (1 - lev), 1)
    half = blocks // 2
    here = one_hot(2 * lax.broadcasted_iota(jnp.int32, (half, blocks), 0) + lev == at)
    names = lax.broadcasted_iota(jnp.int32, (SUB, blocks), 1).astype(jnp.float32)
    order_ref[...] = contract_last(names.astype(jnp.bfloat16), here).astype(jnp.int32)
    source = src_ref[...]
    digits = [lax.shift_right_logical(source, 5), jnp.bitwise_and(source, 31)]
    moved = [contract_last(here, d.astype(jnp.float32).astype(jnp.bfloat16)) for d in digits]
    cells_ref[...] = (moved[0] * 32.0 + moved[1]).astype(jnp.int32)

    line = slots * SUB + core * lines + lax.shift_right_logical(turn_at, GROUP_BITS)
    lane = jnp.bitwise_and(turn_at, GROUP - 1)
    cell = tgt_ref[...] + 1
    high = lax.shift_right_logical(cell, 5).astype(jnp.float32)
    low = jnp.bitwise_and(cell, 31).astype(jnp.float32)
    found = [None, None]
    lines = lax.broadcasted_iota(jnp.int32, (count * SUB, blocks), 0) == line
    group = lax.broadcasted_iota(jnp.int32, (LANES, blocks), 0) // TB
    for q in range(GROUP):
        mine = one_hot(jnp.logical_and(lines, lane == q))
        for g, digit in enumerate((high, low)):
            spread = jnp.where(group == q, jnp.concatenate([digit] * GROUP, axis=0), 0.0)
            part = contract_last(mine, spread.astype(jnp.bfloat16))
            found[g] = part if found[g] is None else found[g] + part
    tags_ref[...] = (found[0] * 32.0 + found[1]).astype(jnp.int32) - 1


def prepare_kernel(
    count, lev_count, lines, field_ref, coef_ref, near_ref, dest_ref, tgt_ref, src_ref,
    recon, order_ref, start_ref, tags_ref, cells_ref,
    ext, mixes, out_sem, in_sem, swap_sem,
):
    cells = field_ref.shape[0]
    window = TILE + 2 * HW
    tiles = cells // TILE
    me = lax.axis_index("src")
    lev = lax.axis_index("lev")
    right = lax.rem(me + 1, count)
    left = lax.rem(me + count - 1, count)
    barrier = pltpu.get_barrier_semaphore()
    for other in (left, right):
        for core in range(lev_count):
            pl.semaphore_signal(barrier, inc=1, device_id=(other, core), device_id_type=MESH)
    twin = lax.rem(lev + 1, lev_count)
    pl.semaphore_signal(barrier, inc=1, device_id=(me, twin), device_id_type=MESH)
    ext[lev, HW:HW + cells, :] = field_ref[...]
    pl.semaphore_wait(barrier, 2 * lev_count + 1)
    swap = pltpu.make_async_remote_copy(
        src_ref=field_ref, dst_ref=ext.at[lev, pl.ds(HW, cells)],
        send_sem=swap_sem.at[0], recv_sem=swap_sem.at[1],
        device_id=(me, twin), device_id_type=MESH,
    )
    swap.start()

    def edge(side, core, source):
        return pltpu.make_async_remote_copy(
            src_ref=field_ref.at[pl.ds((1 - side) * (cells - HW), HW)],
            dst_ref=ext.at[source, pl.ds(side * (HW + cells), HW)],
            send_sem=out_sem.at[side, core], recv_sem=in_sem.at[side, source],
            device_id=((right, left)[side], core), device_id_type=MESH,
        )

    for side in range(2):
        for core in range(lev_count):
            edge(side, core, lev).start()
    plan(count, lines, dest_ref, tgt_ref, src_ref, order_ref, start_ref, tags_ref, cells_ref)

    columns = field_ref.shape[1]

    def put(at, parts):
        for h in range(lev_count):
            recon[h, pl.ds(at, TILE, stride=SUB), :] = parts[h].astype(jnp.float32)

    def tile(t):
        base = pl.multiple_of(t * TILE, TILE)
        near = near_ref[:, pl.ds(base, TILE)] - base
        coef = [coef_ref[g, :, pl.ds(base, TILE)] for g in range(2)]
        totals = [-jnp.sum(coef[g], axis=0, keepdims=True) for g in range(2)]
        held = jnp.concatenate(
            [ext[h, pl.ds(base, window), :] for h in range(lev_count)], axis=1
        )
        rows = pl.multiple_of(base * SUB, TILE * SUB)
        put(rows, [ext[h, pl.ds(base + HW, TILE), :] for h in range(lev_count)])
        for w in range(0, window, PIECE):
            here = lax.broadcasted_iota(jnp.int32, (PIECE, TILE), 0) + w
            own = here == lax.broadcasted_iota(jnp.int32, (PIECE, TILE), 1) + HW
            mixed = [jnp.where(own, totals[g], 0.0) for g in range(2)]
            for k in range(near.shape[0]):
                hit = here == near[k:k + 1, :]
                for g in range(2):
                    mixed[g] = mixed[g] + jnp.where(hit, coef[g][k:k + 1, :], 0.0)
            for g in range(2):
                high = mixed[g].astype(jnp.bfloat16)
                rest = (mixed[g] - high.astype(jnp.float32)).astype(jnp.bfloat16)
                mixes[w:w + PIECE, 2 * g * TILE:(2 * g + 1) * TILE] = high
                mixes[w:w + PIECE, (2 * g + 1) * TILE:(2 * g + 2) * TILE] = rest
        for g in range(2):
            value = contract_first(mixes[:, 2 * g * TILE:(2 * g + 1) * TILE], held)
            value = value + contract_first(mixes[:, (2 * g + 1) * TILE:(2 * g + 2) * TILE], held)
            put(rows + 1 + g, [value[:, h * columns:(h + 1) * columns] for h in range(lev_count)])

    swap.wait()

    @pl.loop(1, tiles - 1)
    def _(t):
        tile(t)

    for side in range(2):
        for core in range(lev_count):
            edge(side, core, core).wait()

    @pl.loop(0, 2)
    def _(e):
        tile(e * (tiles - 1))


def prepare(count, lev_count, lines, field, coef, near_t, dest_t, tgt_t, src_t):
    cells, columns = field.shape
    half = dest_t.shape[1] // 2
    vmem = pl.BlockSpec(memory_space=pltpu.VMEM)
    return pl.pallas_call(
        functools.partial(prepare_kernel, count, lev_count, lines),
        out_shape=(
            jax.ShapeDtypeStruct((lev_count, cells * SUB, columns), jnp.float32),
            jax.ShapeDtypeStruct((SUB, half), jnp.int32),
            jax.ShapeDtypeStruct((SUB, max(count, LANES)), jnp.int32),
            jax.ShapeDtypeStruct((count * SUB, LANES), jnp.int32),
            jax.ShapeDtypeStruct((half, src_t.shape[0]), jnp.int32),
        ),
        in_specs=[vmem] * 6,
        out_specs=(vmem,) * 5,
        scratch_shapes=[
            pltpu.VMEM((lev_count, cells + 2 * HW, columns), jnp.bfloat16),
            pltpu.VMEM((TILE + 2 * HW, 4 * TILE), jnp.bfloat16),
            pltpu.SemaphoreType.DMA((2, lev_count)),
            pltpu.SemaphoreType.DMA((2, lev_count)),
            pltpu.SemaphoreType.DMA((2,)),
        ],
        compiler_params=pltpu.CompilerParams(
            vmem_limit_bytes=28 << 20, collective_id=1, has_side_effects=True
        ),
        name="prepare",
    )(field, coef, near_t, dest_t, tgt_t, src_t)


def remap_kernel(
    count, capacity, level_count, lev_count,
    src_ref, order_ref, start_ref, level_ref, recon, weight_ref, tags_ref,
    remapped_ref, sum_ref,
    picked, compact, staged, land, seen, total, dense_out, dense_in, local_sum, other_sum,
    chunk_out, chunk_in, tag_out, tag_in, line_out, line_in, sum_sem,
):
    me = lax.axis_index("src")
    lev = lax.axis_index("lev")
    outer, inner, plane, outers = place(count)
    steps = count // PLANE
    base = me - plane
    rows = capacity * TB
    width = min(LANES, rows)
    lines = rows // width
    targets, columns = total.shape
    twin = lax.rem(lev + 1, lev_count)
    peers = [
        base + PLANE - 1 - plane,
        base + plane + 1 - 2 * lax.rem(plane, 2),
        base + lax.rem(plane + 2, PLANE),
    ]
    partner = me + PLANE * (1 - 2 * inner)

    def mirror(turn):
        return lax.rem(outer + turn, outers) * PLANE * PAIR + inner * PLANE + plane

    barrier = pltpu.get_barrier_semaphore()
    for other in peers:
        for core in range(lev_count):
            pl.semaphore_signal(barrier, inc=1, device_id=(other, core), device_id_type=MESH)
    pl.semaphore_signal(barrier, inc=1, device_id=(partner, lev), device_id_type=MESH)

    @pl.loop(1, outers)
    def _(t):
        pl.semaphore_signal(barrier, inc=1, device_id=(mirror(t), lev), device_id_type=MESH)

    pl.semaphore_signal(barrier, inc=1, device_id=(me, twin), device_id_type=MESH)

    @pl.loop(0, compact.shape[1] // SUB)
    def _(n):
        compact[:, pl.ds(n * SUB, SUB)] = jnp.zeros((lev_count, SUB, TB, columns), jnp.bfloat16)

    seen[PLANE - 1] = tags_ref[PLANE - 1]
    pl.semaphore_wait(barrier, (PLANE - 1) * lev_count + 1 + outers)

    def tag_copy(spot):
        return pltpu.make_async_remote_copy(
            src_ref=tags_ref.at[spot], dst_ref=seen.at[spot],
            send_sem=tag_out.at[spot], recv_sem=tag_in.at[spot],
            device_id=(peers[spot], lev), device_id_type=MESH,
        )

    def chunk_copy(step, spot, core, source):
        return pltpu.make_async_remote_copy(
            src_ref=staged.at[step, spot, core], dst_ref=land.at[step, spot, source],
            send_sem=chunk_out.at[step, spot, core], recv_sem=chunk_in.at[step, spot, source],
            device_id=((peers + [me])[spot], core), device_id_type=MESH,
        )

    def line_copy(step, to):
        return pltpu.make_async_remote_copy(
            src_ref=dense_out.at[step], dst_ref=dense_in.at[step],
            send_sem=line_out.at[step], recv_sem=line_in.at[step],
            device_id=(to, lev), device_id_type=MESH,
        )

    for spot in range(PLANE - 1):
        tag_copy(spot).start()

    def fetch(first, unroll):
        for begin in range(0, SB, BATCH):
            for m in range(unroll):
                index = src_ref.at[first + m]
                buffer = picked.at[m]
                found = [
                    [recon[h, index[begin + j]] for h in range(lev_count)] for j in range(BATCH)
                ]
                for j in range(BATCH):
                    to = ((begin + j) % GROUP) * (SB // GROUP) + (begin + j) // GROUP
                    for h in range(lev_count):
                        buffer[h, pl.ds(to, 3, stride=SPAN), :] = found[j][h][0:3, :]

    def one(i, buffer):
        held = weight_ref[order_ref[0, i]]
        whole = None
        for q in range(GROUP):
            sides = []
            for h in range(lev_count):
                parts = [
                    buffer[h, pl.ds(c * SPAN + q * (SB // GROUP), SB // GROUP), :]
                    for c in range(3)
                ]
                sides.append(jnp.concatenate(parts, axis=0).astype(jnp.bfloat16))
            terms = jnp.concatenate(sides, axis=1)
            product = contract_first(held[:, q * TB:(q + 1) * TB], terms)
            whole = product if whole is None else whole + product
        for h in range(lev_count):
            compact[h, i] = whole[:, h * columns:(h + 1) * columns].astype(jnp.bfloat16)

    def stage(step, spot):
        first = start_ref[0, step * PLANE + spot]
        if spot < PLANE - 1:
            for core in range(lev_count):
                staged[step, spot, core] = compact[core, pl.ds(first, capacity)].reshape(
                    rows, columns
                )
                chunk_copy(step, spot, core, lev).start()
        else:
            land[step, spot, lev] = compact[lev, pl.ds(first, capacity)].reshape(rows, columns)
            staged[step, spot, twin] = compact[twin, pl.ds(first, capacity)].reshape(rows, columns)
            chunk_copy(step, spot, twin, lev).start()

    unroll = min(UNROLL, capacity)

    @pl.loop(0, steps // 2)
    def _(step):
        for spot in range(PLANE):

            @pl.loop(0, capacity // unroll)
            def _(n, spot=spot):
                first = (step * PLANE + spot) * capacity + n * unroll
                fetch(first, unroll)
                for m in range(unroll):
                    one(first + m, picked.at[m])

            stage(step, spot)

    @pl.loop(steps // 2, steps)
    def _(step):
        for spot in range(PLANE):
            stage(step, spot)

    for spot in range(PLANE - 1):
        tag_copy(spot).wait_recv()

    def add(step, spot, fresh):
        cell = seen[spot, step]
        part = lax.shift_right_arithmetic(cell, 8)
        low = jnp.bitwise_and(cell, BAND - 1)
        chunk = land[step, spot].reshape(lev_count * rows, columns)
        where = lax.broadcasted_iota(jnp.int32, (BAND, width), 0).astype(jnp.float32)
        where = where.astype(jnp.bfloat16)
        for h in range(targets // BAND):
            mark = jnp.where(part == h, low, -1).astype(jnp.float32).astype(jnp.bfloat16)
            hits = jnp.concatenate(
                [one_hot(where == mark[m:m + 1, :width]) for m in range(lev_count * lines)], axis=1
            )
            sums = jnp.dot(hits, chunk, preferred_element_type=jnp.float32)
            band = pl.ds(h * BAND, BAND)
            total[band, :] = sums if fresh else total[band, :] + sums

    def gather(step):
        chunk_copy(step, PLANE - 1, twin, twin).wait_recv()
        add(step, PLANE - 1, True)
        for spot in range(PLANE - 1):
            for core in range(lev_count):
                chunk_copy(step, spot, core, core).wait_recv()
            add(step, spot, False)

    def near(step):
        gather(step)
        dense_out[step] = total[...].astype(jnp.bfloat16)
        line_copy(step, partner).start()

    @pl.loop(0, outers - 1)
    def _(turn):
        step = 2 * turn
        near(step)
        gather(step + 1)
        line_copy(step, partner).wait_recv()
        both = total[...] + dense_in[step].astype(jnp.float32)
        dense_out[step + 1] = both.astype(jnp.bfloat16)
        line_copy(step + 1, mirror(turn + 1)).start()

    near(steps - 2)
    gather(steps - 1)
    line_copy(steps - 2, partner).wait_recv()
    total[...] += dense_in[steps - 2].astype(jnp.float32)

    @pl.loop(0, outers - 1)
    def _(turn):
        line_copy(2 * turn + 1, mirror(turn + 1)).wait_recv()
        total[...] += dense_in[2 * turn + 1].astype(jnp.float32)

    result = total[...]
    remapped_ref[...] = result.astype(jnp.bfloat16)
    start = lev * level_count
    which = lax.broadcasted_iota(jnp.int32, (FIELDS, columns), 1)
    line = lax.broadcasted_iota(jnp.int32, (FIELDS, columns), 0)
    mix = jnp.zeros((FIELDS, columns), jnp.float32)
    for l in range(level_count):
        mix = jnp.where(which == line + l * FIELDS, level_ref[start + l], mix)
    local_sum[...] = lax.dot_general(
        mix,
        result,
        (((1,), (1,)), ((), ())),
        precision=lax.Precision.HIGHEST,
        preferred_element_type=jnp.float32,
    )
    swap = pltpu.make_async_remote_copy(
        src_ref=local_sum, dst_ref=other_sum, send_sem=sum_sem.at[0], recv_sem=sum_sem.at[1],
        device_id=(me, twin), device_id_type=MESH,
    )
    swap.start()
    for spot in range(PLANE - 1):
        tag_copy(spot).wait_send()

    @pl.loop(0, steps)
    def _(step):
        for spot in range(PLANE - 1):
            for core in range(lev_count):
                chunk_copy(step, spot, core, lev).wait_send()
        chunk_copy(step, PLANE - 1, twin, lev).wait_send()

    @pl.loop(0, steps - 1)
    def _(step):
        line_copy(step, partner).wait_send()

    swap.wait()
    sum_ref[...] = local_sum[...] + other_sum[...]


def remap(count, capacity, lev_count, level_count, cells, order, start, level, recon, weight, tags):
    columns = recon.shape[3]
    blocks = cells.shape[0]
    steps = count // PLANE
    rows = capacity * TB
    smem = pl.BlockSpec(memory_space=pltpu.SMEM)
    vmem = pl.BlockSpec(memory_space=pltpu.VMEM)
    dma = pltpu.SemaphoreType.DMA
    chunk = (lev_count, rows, columns)
    dense = (T_DEV, columns)
    return pl.pallas_call(
        functools.partial(remap_kernel, count, capacity, level_count, lev_count),
        out_shape=(
            jax.ShapeDtypeStruct(dense, jnp.bfloat16),
            jax.ShapeDtypeStruct((FIELDS, T_DEV), jnp.float32),
        ),
        in_specs=[smem] * 4 + [vmem] * 3,
        out_specs=(vmem, vmem),
        scratch_shapes=[
            pltpu.VMEM((UNROLL, lev_count, 3 * SPAN, columns), jnp.float32),
            pltpu.VMEM((lev_count, -(-(blocks + capacity) // SUB) * SUB, TB, columns), jnp.bfloat16),
            pltpu.VMEM((steps, PLANE) + chunk, jnp.bfloat16),
            pltpu.VMEM((steps, PLANE) + chunk, jnp.bfloat16),
            pltpu.VMEM((PLANE, steps, SUB, LANES), jnp.int32),
            pltpu.VMEM(dense, jnp.float32),
            pltpu.VMEM((steps - 1,) + dense, jnp.bfloat16),
            pltpu.VMEM((steps - 1,) + dense, jnp.bfloat16),
            pltpu.VMEM((FIELDS, T_DEV), jnp.float32),
            pltpu.VMEM((FIELDS, T_DEV), jnp.float32),
            dma((steps, PLANE, lev_count)),
            dma((steps, PLANE, lev_count)),
            dma((PLANE - 1,)),
            dma((PLANE - 1,)),
            dma((steps - 1,)),
            dma((steps - 1,)),
            dma((2,)),
        ],
        compiler_params=pltpu.CompilerParams(
            vmem_limit_bytes=(16 << 20) + steps * (3 << 18), collective_id=0, has_side_effects=True
        ),
        name="remap",
    )(cells, order, start, level, recon, weight, tags)


def shards(field, grad_coef, neighbours, level_weight, src_index, tgt_index, block_dest, weights):
    count = lax.axis_size("src")
    columns = field.shape[1]
    blocks = src_index.shape[0]
    lev_count = lax.axis_size("lev")
    capacity = 2 * blocks // count // lev_count
    lines = -(-capacity // GROUP)
    steps = count // PLANE
    shaped = weights.reshape(blocks, 3 * SB * TB // LANES, LANES)
    recon, order, start, tags, cells = prepare(
        count, lev_count, lines, field, grad_coef, neighbours.T, block_dest.T, tgt_index.T,
        src_index.T,
    )
    return remap(
        count, capacity, lev_count, columns // FIELDS, cells, order, start,
        level_weight, recon.reshape(lev_count, -1, SUB, columns), shaped, tags.reshape(PLANE, steps, SUB, LANES),
    )


def solution(mesh):
    placed = (
        P("src", "lev"),
        P(None, None, "src"),
        P("src", None),
        P(),
        P("src", None),
        P("src", None),
        P("src", None),
        P("src", None),
    )
    return jax.shard_map(
        shards,
        mesh=mesh,
        in_specs=placed,
        out_specs=(P("src", "lev"), P(None, "src")),
        check_vma=False,
    )
```

```python
import functools

import jax
import jax.numpy as jnp
from jax import lax
from jax.experimental import pallas as pl
from jax.experimental.pallas import tpu as pltpu
from jax.sharding import PartitionSpec as P

FIELDS = 32
HW = 64
SB = 64
TB = 32
T_DEV = 1024
LANES = 128
SUB = 8
TILE = 128
GROUP = LANES // TB
GROUP_BITS = GROUP.bit_length() - 1
PIECE = 32
UNROLL = 4
BATCH = 16
SPAN = SB + SUB
PLANE = 4
PAIR = 2
BAND = 256
MESH = pl.DeviceIdType.MESH


def contract_first(a, b):
    return lax.dot_general(a, b, (((0,), (0,)), ((), ())), preferred_element_type=jnp.float32)


def contract_last(a, b):
    return lax.dot_general(a, b, (((1,), (1,)), ((), ())), preferred_element_type=jnp.float32)


def place(count):
    me = lax.axis_index("src")
    column = PLANE * PAIR
    return me // column, lax.rem(me // PLANE, PAIR), lax.rem(me, PLANE), count // column


def one_hot(mask):
    return jnp.where(mask, jnp.bfloat16(1), jnp.bfloat16(0))


def plan(count, lines, dest_ref, tgt_ref, src_ref, order_ref, start_ref, tags_ref, cells_ref):
    lev = lax.axis_index("lev")
    blocks = dest_ref.shape[1]
    outer, inner, plane, outers = place(count)
    steps = count // PLANE
    owner = dest_ref[...]
    turn = lax.shift_right_logical(owner, 3) - outer - 1
    turn = jnp.where(turn < 0, turn + outers, turn)
    same = jnp.bitwise_and(lax.shift_right_logical(owner, 2), 1) == inner
    step = 2 * turn + jnp.where(same, 1, 0)
    apart = jnp.bitwise_xor(jnp.bitwise_and(owner, PLANE - 1), plane)
    spot = jnp.where(apart == 3, 0, jnp.where(apart == 0, 3, apart))
    key = step * PLANE + spot
    slots = spot * steps + step

    keys = max(count, LANES)
    rows = lax.broadcasted_iota(jnp.int32, (keys, blocks), 0)
    hit = rows == key
    ones = one_hot(hit)
    before = one_hot(
        lax.broadcasted_iota(jnp.int32, (blocks, blocks), 0)
        < lax.broadcasted_iota(jnp.int32, (blocks, blocks), 1)
    )
    less = one_hot(
        lax.broadcasted_iota(jnp.int32, (keys, keys), 1)
        < lax.broadcasted_iota(jnp.int32, (keys, keys), 0)
    )
    prefix = jnp.dot(ones, before, preferred_element_type=jnp.float32)
    ahead = jnp.dot(less, ones, preferred_element_type=jnp.float32)
    starts = jnp.sum(ahead, axis=1, keepdims=True)
    rank = jnp.sum(jnp.where(hit, prefix, 0.0), axis=0, keepdims=True).astype(jnp.int32)
    first = jnp.sum(jnp.where(hit, starts, 0.0), axis=0, keepdims=True).astype(jnp.int32)
    at = rank + first
    core = jnp.bitwise_and(at, 1)
    turn_at = lax.shift_right_logical(at, 1) - lax.shift_right_logical(first + 1 - core, 1)
    every = contract_last(jnp.ones((SUB, blocks), jnp.bfloat16), ahead.astype(jnp.bfloat16))
    start_ref[...] = lax.shift_right_logical(every.astype(jnp.int32) + (1 - lev), 1)
    half = blocks // 2
    here = one_hot(2 * lax.broadcasted_iota(jnp.int32, (half, blocks), 0) + lev == at)
    names = lax.broadcasted_iota(jnp.int32, (SUB, blocks), 1).astype(jnp.float32)
    order_ref[...] = contract_last(names.astype(jnp.bfloat16), here).astype(jnp.int32)
    source = src_ref[...]
    digits = [lax.shift_right_logical(source, 5), jnp.bitwise_and(source, 31)]
    moved = [contract_last(here, d.astype(jnp.float32).astype(jnp.bfloat16)) for d in digits]
    cells_ref[...] = (moved[0] * 32.0 + moved[1]).astype(jnp.int32)

    line = slots * SUB + core * lines + lax.shift_right_logical(turn_at, GROUP_BITS)
    lane = jnp.bitwise_and(turn_at, GROUP - 1)
    cell = tgt_ref[...] + 1
    high = lax.shift_right_logical(cell, 5).astype(jnp.float32)
    low = jnp.bitwise_and(cell, 31).astype(jnp.float32)
    found = [None, None]
    lines = lax.broadcasted_iota(jnp.int32, (count * SUB, blocks), 0) == line
    group = lax.broadcasted_iota(jnp.int32, (LANES, blocks), 0) // TB
    for q in range(GROUP):
        mine = one_hot(jnp.logical_and(lines, lane == q))
        for g, digit in enumerate((high, low)):
            spread = jnp.where(group == q, jnp.concatenate([digit] * GROUP, axis=0), 0.0)
            part = contract_last(mine, spread.astype(jnp.bfloat16))
            found[g] = part if found[g] is None else found[g] + part
    tags_ref[...] = (found[0] * 32.0 + found[1]).astype(jnp.int32) - 1


def prepare_kernel(
    count, lev_count, lines, field_ref, coef_ref, near_ref, dest_ref, tgt_ref, src_ref,
    recon, order_ref, start_ref, tags_ref, cells_ref,
    ext, mixes, out_sem, in_sem, swap_sem,
):
    cells = field_ref.shape[0]
    window = TILE + 2 * HW
    tiles = cells // TILE
    me = lax.axis_index("src")
    lev = lax.axis_index("lev")
    right = lax.rem(me + 1, count)
    left = lax.rem(me + count - 1, count)
    barrier = pltpu.get_barrier_semaphore()
    for other in (left, right):
        for core in range(lev_count):
            pl.semaphore_signal(barrier, inc=1, device_id=(other, core), device_id_type=MESH)
    twin = lax.rem(lev + 1, lev_count)
    pl.semaphore_signal(barrier, inc=1, device_id=(me, twin), device_id_type=MESH)
    ext[lev, HW:HW + cells, :] = field_ref[...]
    pl.semaphore_wait(barrier, 2 * lev_count + 1)
    swap = pltpu.make_async_remote_copy(
        src_ref=field_ref, dst_ref=ext.at[lev, pl.ds(HW, cells)],
        send_sem=swap_sem.at[0], recv_sem=swap_sem.at[1],
        device_id=(me, twin), device_id_type=MESH,
    )
    swap.start()

    def edge(side, core, source):
        return pltpu.make_async_remote_copy(
            src_ref=field_ref.at[pl.ds((1 - side) * (cells - HW), HW)],
            dst_ref=ext.at[source, pl.ds(side * (HW + cells), HW)],
            send_sem=out_sem.at[side, core], recv_sem=in_sem.at[side, source],
            device_id=((right, left)[side], core), device_id_type=MESH,
        )

    for side in range(2):
        for core in range(lev_count):
            edge(side, core, lev).start()
    plan(count, lines, dest_ref, tgt_ref, src_ref, order_ref, start_ref, tags_ref, cells_ref)

    columns = field_ref.shape[1]

    def put(at, parts):
        for h in range(lev_count):
            recon[h, pl.ds(at, TILE, stride=SUB), :] = parts[h].astype(jnp.float32)

    def tile(t):
        base = pl.multiple_of(t * TILE, TILE)
        near = near_ref[:, pl.ds(base, TILE)] - base
        coef = [coef_ref[g, :, pl.ds(base, TILE)] for g in range(2)]
        totals = [-jnp.sum(coef[g], axis=0, keepdims=True) for g in range(2)]
        held = jnp.concatenate(
            [ext[h, pl.ds(base, window), :] for h in range(lev_count)], axis=1
        )
        rows = pl.multiple_of(base * SUB, TILE * SUB)
        put(rows, [ext[h, pl.ds(base + HW, TILE), :] for h in range(lev_count)])
        for w in range(0, window, PIECE):
            here = lax.broadcasted_iota(jnp.int32, (PIECE, TILE), 0) + w
            own = here == lax.broadcasted_iota(jnp.int32, (PIECE, TILE), 1) + HW
            mixed = [jnp.where(own, totals[g], 0.0) for g in range(2)]
            for k in range(near.shape[0]):
                hit = here == near[k:k + 1, :]
                for g in range(2):
                    mixed[g] = mixed[g] + jnp.where(hit, coef[g][k:k + 1, :], 0.0)
            for g in range(2):
                high = mixed[g].astype(jnp.bfloat16)
                rest = (mixed[g] - high.astype(jnp.float32)).astype(jnp.bfloat16)
                mixes[w:w + PIECE, 2 * g * TILE:(2 * g + 1) * TILE] = high
                mixes[w:w + PIECE, (2 * g + 1) * TILE:(2 * g + 2) * TILE] = rest
        for g in range(2):
            value = contract_first(mixes[:, 2 * g * TILE:(2 * g + 1) * TILE], held)
            value = value + contract_first(mixes[:, (2 * g + 1) * TILE:(2 * g + 2) * TILE], held)
            put(rows + 1 + g, [value[:, h * columns:(h + 1) * columns] for h in range(lev_count)])

    swap.wait()

    @pl.loop(1, tiles - 1)
    def _(t):
        tile(t)

    for side in range(2):
        for core in range(lev_count):
            edge(side, core, core).wait()

    @pl.loop(0, 2)
    def _(e):
        tile(e * (tiles - 1))


def prepare(count, lev_count, lines, field, coef, near_t, dest_t, tgt_t, src_t):
    cells, columns = field.shape
    half = dest_t.shape[1] // 2
    vmem = pl.BlockSpec(memory_space=pltpu.VMEM)
    return pl.pallas_call(
        functools.partial(prepare_kernel, count, lev_count, lines),
        out_shape=(
            jax.ShapeDtypeStruct((lev_count, cells * SUB, columns), jnp.float32),
            jax.ShapeDtypeStruct((SUB, half), jnp.int32),
            jax.ShapeDtypeStruct((SUB, max(count, LANES)), jnp.int32),
            jax.ShapeDtypeStruct((count * SUB, LANES), jnp.int32),
            jax.ShapeDtypeStruct((half, src_t.shape[0]), jnp.int32),
        ),
        in_specs=[vmem] * 6,
        out_specs=(vmem,) * 5,
        scratch_shapes=[
            pltpu.VMEM((lev_count, cells + 2 * HW, columns), jnp.bfloat16),
            pltpu.VMEM((TILE + 2 * HW, 4 * TILE), jnp.bfloat16),
            pltpu.SemaphoreType.DMA((2, lev_count)),
            pltpu.SemaphoreType.DMA((2, lev_count)),
            pltpu.SemaphoreType.DMA((2,)),
        ],
        compiler_params=pltpu.CompilerParams(
            vmem_limit_bytes=28 << 20, collective_id=1, has_side_effects=True
        ),
        name="prepare",
    )(field, coef, near_t, dest_t, tgt_t, src_t)


def remap_kernel(
    count, capacity, level_count, lev_count,
    src_ref, order_ref, start_ref, level_ref, recon, weight_ref, tags_ref,
    remapped_ref, sum_ref,
    picked, compact, staged, land, seen, total, dense_out, dense_in, local_sum, other_sum,
    chunk_out, chunk_in, tag_out, tag_in, line_out, line_in, sum_out, sum_in,
):
    me = lax.axis_index("src")
    lev = lax.axis_index("lev")
    outer, inner, plane, outers = place(count)
    steps = count // PLANE
    base = me - plane
    rows = capacity * TB
    width = min(LANES, rows)
    lines = rows // width
    bands, _, columns = remapped_ref.shape
    twin = lax.rem(lev + 1, lev_count)
    peers = [
        base + PLANE - 1 - plane,
        base + plane + 1 - 2 * lax.rem(plane, 2),
        base + lax.rem(plane + 2, PLANE),
    ]
    partner = me + PLANE * (1 - 2 * inner)

    def mirror(turn):
        return lax.rem(outer + turn, outers) * PLANE * PAIR + inner * PLANE + plane

    barrier = pltpu.get_barrier_semaphore()
    for other in peers:
        for core in range(lev_count):
            pl.semaphore_signal(barrier, inc=1, device_id=(other, core), device_id_type=MESH)
    pl.semaphore_signal(barrier, inc=1, device_id=(partner, lev), device_id_type=MESH)

    @pl.loop(1, outers)
    def _(t):
        pl.semaphore_signal(barrier, inc=1, device_id=(mirror(t), lev), device_id_type=MESH)

    pl.semaphore_signal(barrier, inc=1, device_id=(me, twin), device_id_type=MESH)

    @pl.loop(0, compact.shape[1] // SUB)
    def _(n):
        compact[:, pl.ds(n * SUB, SUB)] = jnp.zeros((lev_count, SUB, TB, columns), jnp.bfloat16)

    seen[PLANE - 1] = tags_ref[PLANE - 1]
    pl.semaphore_wait(barrier, (PLANE - 1) * lev_count + 1 + outers)

    def tag_copy(spot):
        return pltpu.make_async_remote_copy(
            src_ref=tags_ref.at[spot], dst_ref=seen.at[spot],
            send_sem=tag_out.at[spot], recv_sem=tag_in.at[spot],
            device_id=(peers[spot], lev), device_id_type=MESH,
        )

    def chunk_copy(step, spot, core, source):
        return pltpu.make_async_remote_copy(
            src_ref=staged.at[step, spot, core], dst_ref=land.at[step, spot, source],
            send_sem=chunk_out.at[step, spot, core], recv_sem=chunk_in.at[step, spot, source],
            device_id=((peers + [me])[spot], core), device_id_type=MESH,
        )

    def line_copy(step, band, to):
        return pltpu.make_async_remote_copy(
            src_ref=dense_out.at[step, band], dst_ref=dense_in.at[step, band],
            send_sem=line_out.at[step, band], recv_sem=line_in.at[step, band],
            device_id=(to, lev), device_id_type=MESH,
        )

    def swap(band):
        return pltpu.make_async_remote_copy(
            src_ref=local_sum.at[band], dst_ref=other_sum.at[band],
            send_sem=sum_out.at[band], recv_sem=sum_in.at[band],
            device_id=(me, twin), device_id_type=MESH,
        )

    for spot in range(PLANE - 1):
        tag_copy(spot).start()

    def fetch(first, unroll):
        for begin in range(0, SB, BATCH):
            for m in range(unroll):
                index = src_ref.at[first + m]
                buffer = picked.at[m]
                found = [
                    [recon[h, index[begin + j]] for h in range(lev_count)] for j in range(BATCH)
                ]
                for j in range(BATCH):
                    to = ((begin + j) % GROUP) * (SB // GROUP) + (begin + j) // GROUP
                    for h in range(lev_count):
                        buffer[h, pl.ds(to, 3, stride=SPAN), :] = found[j][h][0:3, :]

    def one(i, buffer):
        held = weight_ref[order_ref[0, i]]
        whole = None
        for q in range(GROUP):
            sides = []
            for h in range(lev_count):
                parts = [
                    buffer[h, pl.ds(c * SPAN + q * (SB // GROUP), SB // GROUP), :]
                    for c in range(3)
                ]
                sides.append(jnp.concatenate(parts, axis=0).astype(jnp.bfloat16))
            terms = jnp.concatenate(sides, axis=1)
            product = contract_first(held[:, q * TB:(q + 1) * TB], terms)
            whole = product if whole is None else whole + product
        for h in range(lev_count):
            compact[h, i] = whole[:, h * columns:(h + 1) * columns].astype(jnp.bfloat16)

    def stage(step, spot):
        first = start_ref[0, step * PLANE + spot]
        if spot < PLANE - 1:
            for core in range(lev_count):
                staged[step, spot, core] = compact[core, pl.ds(first, capacity)].reshape(
                    rows, columns
                )
                chunk_copy(step, spot, core, lev).start()
        else:
            land[step, spot, lev] = compact[lev, pl.ds(first, capacity)].reshape(rows, columns)
            staged[step, spot, twin] = compact[twin, pl.ds(first, capacity)].reshape(rows, columns)
            chunk_copy(step, spot, twin, lev).start()

    unroll = min(UNROLL, capacity)

    @pl.loop(0, steps // 2)
    def _(step):
        for spot in range(PLANE):

            @pl.loop(0, capacity // unroll)
            def _(n, spot=spot):
                first = (step * PLANE + spot) * capacity + n * unroll
                fetch(first, unroll)
                for m in range(unroll):
                    one(first + m, picked.at[m])

            stage(step, spot)

    def stage_all(step):
        for spot in range(PLANE):
            stage(step, spot)

    @pl.loop(steps // 2, steps - 1)
    def _(step):
        stage_all(step)

    for spot in range(PLANE - 1):
        tag_copy(spot).wait_recv()

    def ready(step):
        for spot in range(PLANE - 1):
            for core in range(lev_count):
                chunk_copy(step, spot, core, core).wait_recv()
        chunk_copy(step, PLANE - 1, twin, twin).wait_recv()

    def gather(step, band):
        where = lax.broadcasted_iota(jnp.int32, (BAND, width), 0).astype(jnp.float32)
        where = where.astype(jnp.bfloat16)
        sums = None
        for spot in range(PLANE):
            cell = seen[spot, step]
            part = lax.shift_right_arithmetic(cell, 8)
            low = jnp.bitwise_and(cell, BAND - 1)
            chunk = land[step, spot].reshape(lev_count * rows, columns)
            mark = jnp.where(part == band, low, -1).astype(jnp.float32).astype(jnp.bfloat16)
            hits = jnp.concatenate(
                [one_hot(where == mark[m:m + 1, :width]) for m in range(lev_count * lines)], axis=1
            )
            term = jnp.dot(hits, chunk, preferred_element_type=jnp.float32)
            sums = term if sums is None else sums + term
        return sums

    def near(step):
        ready(step)

        @pl.loop(0, bands)
        def _(band):
            dense_out[step, band] = gather(step, band).astype(jnp.bfloat16)
            line_copy(step, band, partner).start()

    @pl.loop(0, outers - 1)
    def _(turn):
        step = 2 * turn
        near(step)
        ready(step + 1)

        @pl.loop(0, bands)
        def _(band):
            @pl.when(jnp.logical_and(turn == 0, band == bands // 2))
            def _():
                stage_all(steps - 1)

            sums = gather(step + 1, band)
            line_copy(step, band, partner).wait_recv()
            dense_out[step + 1, band] = (
                sums + dense_in[step, band].astype(jnp.float32)
            ).astype(jnp.bfloat16)
            line_copy(step + 1, band, mirror(turn + 1)).start()

    near(steps - 2)
    ready(steps - 1)
    start = lev * level_count
    which = lax.broadcasted_iota(jnp.int32, (FIELDS, columns), 1)
    line = lax.broadcasted_iota(jnp.int32, (FIELDS, columns), 0)
    mix = jnp.zeros((FIELDS, columns), jnp.float32)
    for l in range(level_count):
        mix = jnp.where(which == line + l * FIELDS, level_ref[start + l], mix)

    @pl.loop(0, bands)
    def _(band):
        total[...] = gather(steps - 1, band)
        line_copy(steps - 2, band, partner).wait_recv()
        total[...] += dense_in[steps - 2, band].astype(jnp.float32)

        @pl.loop(0, outers - 1)
        def _(turn):
            line_copy(2 * turn + 1, band, mirror(turn + 1)).wait_recv()
            total[...] += dense_in[2 * turn + 1, band].astype(jnp.float32)

        result = total[...]
        remapped_ref[band] = result.astype(jnp.bfloat16)
        local_sum[band] = lax.dot_general(
            mix,
            result,
            (((1,), (1,)), ((), ())),
            precision=lax.Precision.HIGHEST,
            preferred_element_type=jnp.float32,
        )
        swap(band).start()

    for spot in range(PLANE - 1):
        tag_copy(spot).wait_send()

    @pl.loop(0, steps)
    def _(step):
        for spot in range(PLANE - 1):
            for core in range(lev_count):
                chunk_copy(step, spot, core, lev).wait_send()
        chunk_copy(step, PLANE - 1, twin, lev).wait_send()

    @pl.loop(0, steps - 1)
    def _(step):
        for band in range(bands):
            line_copy(step, band, partner).wait_send()

    for band in range(bands):
        swap(band).wait()
        sum_ref[:, band * BAND:(band + 1) * BAND] = local_sum[band] + other_sum[band]


def remap(count, capacity, lev_count, level_count, cells, order, start, level, recon, weight, tags):
    columns = recon.shape[3]
    blocks = cells.shape[0]
    steps = count // PLANE
    rows = capacity * TB
    smem = pl.BlockSpec(memory_space=pltpu.SMEM)
    vmem = pl.BlockSpec(memory_space=pltpu.VMEM)
    dma = pltpu.SemaphoreType.DMA
    chunk = (lev_count, rows, columns)
    bands = T_DEV // BAND
    dense = (bands, BAND, columns)
    return pl.pallas_call(
        functools.partial(remap_kernel, count, capacity, level_count, lev_count),
        out_shape=(
            jax.ShapeDtypeStruct(dense, jnp.bfloat16),
            jax.ShapeDtypeStruct((FIELDS, T_DEV), jnp.float32),
        ),
        in_specs=[smem] * 4 + [vmem] * 3,
        out_specs=(vmem, vmem),
        scratch_shapes=[
            pltpu.VMEM((UNROLL, lev_count, 3 * SPAN, columns), jnp.float32),
            pltpu.VMEM((lev_count, -(-(blocks + capacity) // SUB) * SUB, TB, columns), jnp.bfloat16),
            pltpu.VMEM((steps, PLANE) + chunk, jnp.bfloat16),
            pltpu.VMEM((steps, PLANE) + chunk, jnp.bfloat16),
            pltpu.VMEM((PLANE, steps, SUB, LANES), jnp.int32),
            pltpu.VMEM((BAND, columns), jnp.float32),
            pltpu.VMEM((steps - 1,) + dense, jnp.bfloat16),
            pltpu.VMEM((steps - 1,) + dense, jnp.bfloat16),
            pltpu.VMEM((bands, FIELDS, BAND), jnp.float32),
            pltpu.VMEM((bands, FIELDS, BAND), jnp.float32),
            dma((steps, PLANE, lev_count)),
            dma((steps, PLANE, lev_count)),
            dma((PLANE - 1,)),
            dma((PLANE - 1,)),
            dma((steps - 1, bands)),
            dma((steps - 1, bands)),
            dma((bands,)),
            dma((bands,)),
        ],
        compiler_params=pltpu.CompilerParams(
            vmem_limit_bytes=(16 << 20) + steps * (3 << 18), collective_id=0, has_side_effects=True
        ),
        name="remap",
    )(cells, order, start, level, recon, weight, tags)


def shards(field, grad_coef, neighbours, level_weight, src_index, tgt_index, block_dest, weights):
    count = lax.axis_size("src")
    columns = field.shape[1]
    blocks = src_index.shape[0]
    lev_count = lax.axis_size("lev")
    capacity = 2 * blocks // count // lev_count
    lines = -(-capacity // GROUP)
    steps = count // PLANE
    shaped = weights.reshape(blocks, 3 * SB * TB // LANES, LANES)
    recon, order, start, tags, cells = prepare(
        count, lev_count, lines, field, grad_coef, neighbours.T, block_dest.T, tgt_index.T,
        src_index.T,
    )
    remapped, sums = remap(
        count, capacity, lev_count, columns // FIELDS, cells, order, start,
        level_weight, recon.reshape(lev_count, -1, SUB, columns), shaped, tags.reshape(PLANE, steps, SUB, LANES),
    )
    return remapped.reshape(T_DEV, columns), sums


def solution(mesh):
    placed = (
        P("src", "lev"),
        P(None, None, "src"),
        P("src", None),
        P(),
        P("src", None),
        P("src", None),
        P("src", None),
        P("src", None),
    )
    return jax.shard_map(
        shards,
        mesh=mesh,
        in_specs=placed,
        out_specs=(P("src", "lev"), P(None, "src")),
        check_vma=False,
    )
```

```python
import functools

import jax
import jax.numpy as jnp
from jax import lax
from jax.experimental import pallas as pl
from jax.experimental.pallas import tpu as pltpu
from jax.sharding import PartitionSpec as P

FIELDS = 32
HW = 64
SB = 64
TB = 32
T_DEV = 1024
LANES = 128
SUB = 8
TILE = 128
GROUP = LANES // TB
GROUP_BITS = GROUP.bit_length() - 1
PIECE = 32
UNROLL = 4
BATCH = 16
SPAN = SB + SUB
PLANE = 4
PAIR = 2
BAND = 256
MESH = pl.DeviceIdType.MESH


def contract_first(a, b):
    return lax.dot_general(a, b, (((0,), (0,)), ((), ())), preferred_element_type=jnp.float32)


def contract_last(a, b):
    return lax.dot_general(a, b, (((1,), (1,)), ((), ())), preferred_element_type=jnp.float32)


def place(count):
    me = lax.axis_index("src")
    column = PLANE * PAIR
    return me // column, lax.rem(me // PLANE, PAIR), lax.rem(me, PLANE), count // column


def one_hot(mask):
    return jnp.where(mask, jnp.bfloat16(1), jnp.bfloat16(0))


def plan(count, lines, dest_ref, tgt_ref, src_ref, order_ref, start_ref, tags_ref, cells_ref):
    lev = lax.axis_index("lev")
    blocks = dest_ref.shape[1]
    outer, inner, plane, outers = place(count)
    steps = count // PLANE
    owner = dest_ref[...]
    turn = lax.shift_right_logical(owner, 3) - outer - 1
    turn = jnp.where(turn < 0, turn + outers, turn)
    same = jnp.bitwise_and(lax.shift_right_logical(owner, 2), 1) == inner
    step = 2 * turn + jnp.where(same, 1, 0)
    apart = jnp.bitwise_xor(jnp.bitwise_and(owner, PLANE - 1), plane)
    spot = jnp.where(apart == 3, 0, jnp.where(apart == 0, 3, apart))
    key = step * PLANE + spot
    slots = spot * steps + step

    keys = max(count, LANES)
    rows = lax.broadcasted_iota(jnp.int32, (keys, blocks), 0)
    hit = rows == key
    ones = one_hot(hit)
    before = one_hot(
        lax.broadcasted_iota(jnp.int32, (blocks, blocks), 0)
        < lax.broadcasted_iota(jnp.int32, (blocks, blocks), 1)
    )
    less = one_hot(
        lax.broadcasted_iota(jnp.int32, (keys, keys), 1)
        < lax.broadcasted_iota(jnp.int32, (keys, keys), 0)
    )
    prefix = jnp.dot(ones, before, preferred_element_type=jnp.float32)
    ahead = jnp.dot(less, ones, preferred_element_type=jnp.float32)
    starts = jnp.sum(ahead, axis=1, keepdims=True)
    rank = jnp.sum(jnp.where(hit, prefix, 0.0), axis=0, keepdims=True).astype(jnp.int32)
    first = jnp.sum(jnp.where(hit, starts, 0.0), axis=0, keepdims=True).astype(jnp.int32)
    at = rank + first
    core = jnp.bitwise_and(at, 1)
    turn_at = lax.shift_right_logical(at, 1) - lax.shift_right_logical(first + 1 - core, 1)
    every = contract_last(jnp.ones((SUB, blocks), jnp.bfloat16), ahead.astype(jnp.bfloat16))
    start_ref[...] = lax.shift_right_logical(every.astype(jnp.int32) + (1 - lev), 1)
    half = blocks // 2
    here = one_hot(2 * lax.broadcasted_iota(jnp.int32, (half, blocks), 0) + lev == at)
    names = lax.broadcasted_iota(jnp.int32, (SUB, blocks), 1).astype(jnp.float32)
    order_ref[...] = contract_last(names.astype(jnp.bfloat16), here).astype(jnp.int32)
    source = src_ref[...]
    digits = [lax.shift_right_logical(source, 5), jnp.bitwise_and(source, 31)]
    moved = [contract_last(here, d.astype(jnp.float32).astype(jnp.bfloat16)) for d in digits]
    cells_ref[...] = (moved[0] * 32.0 + moved[1]).astype(jnp.int32)

    line = slots * SUB + core * lines + lax.shift_right_logical(turn_at, GROUP_BITS)
    lane = jnp.bitwise_and(turn_at, GROUP - 1)
    cell = tgt_ref[...] + 1
    high = lax.shift_right_logical(cell, 5).astype(jnp.float32)
    low = jnp.bitwise_and(cell, 31).astype(jnp.float32)
    found = [None, None]
    lines = lax.broadcasted_iota(jnp.int32, (count * SUB, blocks), 0) == line
    group = lax.broadcasted_iota(jnp.int32, (LANES, blocks), 0) // TB
    for q in range(GROUP):
        mine = one_hot(jnp.logical_and(lines, lane == q))
        for g, digit in enumerate((high, low)):
            spread = jnp.where(group == q, jnp.concatenate([digit] * GROUP, axis=0), 0.0)
            part = contract_last(mine, spread.astype(jnp.bfloat16))
            found[g] = part if found[g] is None else found[g] + part
    tags_ref[...] = (found[0] * 32.0 + found[1]).astype(jnp.int32) - 1


def prepare_kernel(
    count, lev_count, lines, field_ref, coef_ref, near_ref, dest_ref, tgt_ref, src_ref,
    recon, order_ref, start_ref, tags_ref, cells_ref,
    ext, mixes, out_sem, in_sem, swap_sem,
):
    cells = field_ref.shape[0]
    window = TILE + 2 * HW
    tiles = cells // TILE
    me = lax.axis_index("src")
    lev = lax.axis_index("lev")
    right = lax.rem(me + 1, count)
    left = lax.rem(me + count - 1, count)
    barrier = pltpu.get_barrier_semaphore()
    for other in (left, right):
        for core in range(lev_count):
            pl.semaphore_signal(barrier, inc=1, device_id=(other, core), device_id_type=MESH)
    twin = lax.rem(lev + 1, lev_count)
    pl.semaphore_signal(barrier, inc=1, device_id=(me, twin), device_id_type=MESH)
    ext[lev, HW:HW + cells, :] = field_ref[...]
    pl.semaphore_wait(barrier, 2 * lev_count + 1)
    swap = pltpu.make_async_remote_copy(
        src_ref=field_ref, dst_ref=ext.at[lev, pl.ds(HW, cells)],
        send_sem=swap_sem.at[0], recv_sem=swap_sem.at[1],
        device_id=(me, twin), device_id_type=MESH,
    )
    swap.start()

    def edge(side, core, source):
        return pltpu.make_async_remote_copy(
            src_ref=field_ref.at[pl.ds((1 - side) * (cells - HW), HW)],
            dst_ref=ext.at[source, pl.ds(side * (HW + cells), HW)],
            send_sem=out_sem.at[side, core], recv_sem=in_sem.at[side, source],
            device_id=((right, left)[side], core), device_id_type=MESH,
        )

    for side in range(2):
        for core in range(lev_count):
            edge(side, core, lev).start()
    plan(count, lines, dest_ref, tgt_ref, src_ref, order_ref, start_ref, tags_ref, cells_ref)

    columns = field_ref.shape[1]

    def put(at, parts):
        for h in range(lev_count):
            recon[h, pl.ds(at, TILE, stride=SUB), :] = parts[h].astype(jnp.float32)

    def tile(t):
        base = pl.multiple_of(t * TILE, TILE)
        near = near_ref[:, pl.ds(base, TILE)] - base
        coef = [coef_ref[g, :, pl.ds(base, TILE)] for g in range(2)]
        totals = [-jnp.sum(coef[g], axis=0, keepdims=True) for g in range(2)]
        held = jnp.concatenate(
            [ext[h, pl.ds(base, window), :] for h in range(lev_count)], axis=1
        )
        rows = pl.multiple_of(base * SUB, TILE * SUB)
        put(rows, [ext[h, pl.ds(base + HW, TILE), :] for h in range(lev_count)])
        for w in range(0, window, PIECE):
            here = lax.broadcasted_iota(jnp.int32, (PIECE, TILE), 0) + w
            own = here == lax.broadcasted_iota(jnp.int32, (PIECE, TILE), 1) + HW
            mixed = [jnp.where(own, totals[g], 0.0) for g in range(2)]
            for k in range(near.shape[0]):
                hit = here == near[k:k + 1, :]
                for g in range(2):
                    mixed[g] = mixed[g] + jnp.where(hit, coef[g][k:k + 1, :], 0.0)
            for g in range(2):
                high = mixed[g].astype(jnp.bfloat16)
                rest = (mixed[g] - high.astype(jnp.float32)).astype(jnp.bfloat16)
                mixes[w:w + PIECE, 2 * g * TILE:(2 * g + 1) * TILE] = high
                mixes[w:w + PIECE, (2 * g + 1) * TILE:(2 * g + 2) * TILE] = rest
        for g in range(2):
            value = contract_first(mixes[:, 2 * g * TILE:(2 * g + 1) * TILE], held)
            value = value + contract_first(mixes[:, (2 * g + 1) * TILE:(2 * g + 2) * TILE], held)
            put(rows + 1 + g, [value[:, h * columns:(h + 1) * columns] for h in range(lev_count)])

    swap.wait()

    @pl.loop(1, tiles - 1)
    def _(t):
        tile(t)

    for side in range(2):
        for core in range(lev_count):
            edge(side, core, core).wait()

    @pl.loop(0, 2)
    def _(e):
        tile(e * (tiles - 1))


def prepare(count, lev_count, lines, field, coef, near_t, dest_t, tgt_t, src_t):
    cells, columns = field.shape
    half = dest_t.shape[1] // 2
    vmem = pl.BlockSpec(memory_space=pltpu.VMEM)
    return pl.pallas_call(
        functools.partial(prepare_kernel, count, lev_count, lines),
        out_shape=(
            jax.ShapeDtypeStruct((lev_count, cells * SUB, columns), jnp.float32),
            jax.ShapeDtypeStruct((SUB, half), jnp.int32),
            jax.ShapeDtypeStruct((SUB, max(count, LANES)), jnp.int32),
            jax.ShapeDtypeStruct((count * SUB, LANES), jnp.int32),
            jax.ShapeDtypeStruct((half, src_t.shape[0]), jnp.int32),
        ),
        in_specs=[vmem] * 6,
        out_specs=(vmem,) * 5,
        scratch_shapes=[
            pltpu.VMEM((lev_count, cells + 2 * HW, columns), jnp.bfloat16),
            pltpu.VMEM((TILE + 2 * HW, 4 * TILE), jnp.bfloat16),
            pltpu.SemaphoreType.DMA((2, lev_count)),
            pltpu.SemaphoreType.DMA((2, lev_count)),
            pltpu.SemaphoreType.DMA((2,)),
        ],
        compiler_params=pltpu.CompilerParams(
            vmem_limit_bytes=28 << 20, collective_id=1, has_side_effects=True
        ),
        name="prepare",
    )(field, coef, near_t, dest_t, tgt_t, src_t)


def remap_kernel(
    count, capacity, level_count, lev_count,
    src_ref, order_ref, start_ref, level_ref, recon, weight_ref, tags_ref,
    remapped_ref, sum_ref,
    picked, compact, staged, land, seen, total, dense_out, dense_in, local_sum, other_sum,
    chunk_out, chunk_in, tag_out, tag_in, line_out, line_in, sum_out, sum_in,
):
    me = lax.axis_index("src")
    lev = lax.axis_index("lev")
    outer, inner, plane, outers = place(count)
    steps = count // PLANE
    base = me - plane
    rows = capacity * TB
    width = min(LANES, rows)
    lines = rows // width
    bands, _, columns = remapped_ref.shape
    twin = lax.rem(lev + 1, lev_count)
    peers = [
        base + PLANE - 1 - plane,
        base + plane + 1 - 2 * lax.rem(plane, 2),
        base + lax.rem(plane + 2, PLANE),
    ]
    partner = me + PLANE * (1 - 2 * inner)

    def mirror(turn):
        return lax.rem(outer + turn, outers) * PLANE * PAIR + inner * PLANE + plane

    barrier = pltpu.get_barrier_semaphore()
    for other in peers:
        for core in range(lev_count):
            pl.semaphore_signal(barrier, inc=1, device_id=(other, core), device_id_type=MESH)
    pl.semaphore_signal(barrier, inc=1, device_id=(partner, lev), device_id_type=MESH)

    @pl.loop(1, outers)
    def _(t):
        pl.semaphore_signal(barrier, inc=1, device_id=(mirror(t), lev), device_id_type=MESH)

    pl.semaphore_signal(barrier, inc=1, device_id=(me, twin), device_id_type=MESH)

    @pl.loop(0, compact.shape[1] // SUB)
    def _(n):
        compact[:, pl.ds(n * SUB, SUB)] = jnp.zeros((lev_count, SUB, TB, columns), jnp.bfloat16)

    seen[PLANE - 1] = tags_ref[PLANE - 1]
    pl.semaphore_wait(barrier, (PLANE - 1) * lev_count + 1 + outers)

    def tag_copy(spot):
        return pltpu.make_async_remote_copy(
            src_ref=tags_ref.at[spot], dst_ref=seen.at[spot],
            send_sem=tag_out.at[spot], recv_sem=tag_in.at[spot],
            device_id=(peers[spot], lev), device_id_type=MESH,
        )

    def chunk_copy(step, spot, core, source):
        return pltpu.make_async_remote_copy(
            src_ref=staged.at[step, spot, core], dst_ref=land.at[step, spot, source],
            send_sem=chunk_out.at[step, spot, core], recv_sem=chunk_in.at[step, spot, source],
            device_id=((peers + [me])[spot], core), device_id_type=MESH,
        )

    def line_copy(step, band, to):
        return pltpu.make_async_remote_copy(
            src_ref=dense_out.at[step, band], dst_ref=dense_in.at[step, band],
            send_sem=line_out.at[step, band], recv_sem=line_in.at[step, band],
            device_id=(to, lev), device_id_type=MESH,
        )

    def swap(band):
        return pltpu.make_async_remote_copy(
            src_ref=local_sum.at[band], dst_ref=other_sum.at[band],
            send_sem=sum_out.at[band], recv_sem=sum_in.at[band],
            device_id=(me, twin), device_id_type=MESH,
        )

    for spot in range(PLANE - 1):
        tag_copy(spot).start()

    def fetch(first, unroll):
        for begin in range(0, SB, BATCH):
            for m in range(unroll):
                index = src_ref.at[first + m]
                buffer = picked.at[m]
                found = [
                    [recon[h, index[begin + j]] for h in range(lev_count)] for j in range(BATCH)
                ]
                for j in range(BATCH):
                    to = ((begin + j) % GROUP) * (SB // GROUP) + (begin + j) // GROUP
                    for h in range(lev_count):
                        buffer[h, pl.ds(to, 3, stride=SPAN), :] = found[j][h][0:3, :]

    def one(i, buffer):
        held = weight_ref[order_ref[0, i]]
        whole = None
        for q in range(GROUP):
            sides = []
            for h in range(lev_count):
                parts = [
                    buffer[h, pl.ds(c * SPAN + q * (SB // GROUP), SB // GROUP), :]
                    for c in range(3)
                ]
                sides.append(jnp.concatenate(parts, axis=0).astype(jnp.bfloat16))
            terms = jnp.concatenate(sides, axis=1)
            product = contract_first(held[:, q * TB:(q + 1) * TB], terms)
            whole = product if whole is None else whole + product
        for h in range(lev_count):
            compact[h, i] = whole[:, h * columns:(h + 1) * columns].astype(jnp.bfloat16)

    def stage(step, spot):
        first = start_ref[0, step * PLANE + spot]
        if spot < PLANE - 1:
            for core in range(lev_count):
                staged[step, spot, core] = compact[core, pl.ds(first, capacity)].reshape(
                    rows, columns
                )
                chunk_copy(step, spot, core, lev).start()
        else:
            land[step, spot, lev] = compact[lev, pl.ds(first, capacity)].reshape(rows, columns)
            staged[step, spot, twin] = compact[twin, pl.ds(first, capacity)].reshape(rows, columns)
            chunk_copy(step, spot, twin, lev).start()

    unroll = min(UNROLL, capacity)

    @pl.loop(0, steps // 2)
    def _(step):
        for spot in range(PLANE):

            @pl.loop(0, capacity // unroll)
            def _(n, spot=spot):
                first = (step * PLANE + spot) * capacity + n * unroll
                fetch(first, unroll)
                for m in range(unroll):
                    one(first + m, picked.at[m])

            stage(step, spot)

    def stage_all(step):
        for spot in range(PLANE):
            stage(step, spot)

    @pl.loop(steps // 2, steps - 1)
    def _(step):
        stage_all(step)

    for spot in range(PLANE - 1):
        tag_copy(spot).wait_recv()

    def ready(step):
        for spot in range(PLANE - 1):
            for core in range(lev_count):
                chunk_copy(step, spot, core, core).wait_recv()
        chunk_copy(step, PLANE - 1, twin, twin).wait_recv()

    def gather(step, band):
        where = lax.broadcasted_iota(jnp.int32, (BAND, width), 0).astype(jnp.float32)
        where = where.astype(jnp.bfloat16)
        sums = None
        for spot in range(PLANE):
            cell = seen[spot, step]
            part = lax.shift_right_arithmetic(cell, 8)
            low = jnp.bitwise_and(cell, BAND - 1)
            chunk = land[step, spot].reshape(lev_count * rows, columns)
            mark = jnp.where(part == band, low, -1).astype(jnp.float32).astype(jnp.bfloat16)
            hits = jnp.concatenate(
                [one_hot(where == mark[m:m + 1, :width]) for m in range(lev_count * lines)], axis=1
            )
            term = jnp.dot(hits, chunk, preferred_element_type=jnp.float32)
            sums = term if sums is None else sums + term
        return sums

    def near(step):
        ready(step)

        @pl.loop(0, bands)
        def _(band):
            dense_out[step, band] = gather(step, band).astype(jnp.bfloat16)
            line_copy(step, band, partner).start()

    @pl.loop(0, outers - 1)
    def _(turn):
        step = 2 * turn
        near(step)
        ready(step + 1)

        @pl.loop(0, bands)
        def _(band):
            @pl.when(jnp.logical_and(turn == 0, band == bands // 2))
            def _():
                stage_all(steps - 1)

            sums = gather(step + 1, band)
            line_copy(step, band, partner).wait_recv()
            dense_out[step + 1, band] = (
                sums + dense_in[step, band].astype(jnp.float32)
            ).astype(jnp.bfloat16)
            line_copy(step + 1, band, mirror(turn + 1)).start()

    near(steps - 2)
    ready(steps - 1)
    start = lev * level_count
    which = lax.broadcasted_iota(jnp.int32, (FIELDS, columns), 1)
    line = lax.broadcasted_iota(jnp.int32, (FIELDS, columns), 0)
    mix = jnp.zeros((FIELDS, columns), jnp.float32)
    for l in range(level_count):
        mix = jnp.where(which == line + l * FIELDS, level_ref[start + l], mix)

    @pl.loop(0, bands)
    def _(band):
        total[band] = gather(steps - 1, band)

    @pl.loop(0, bands)
    def _(band):
        line_copy(steps - 2, band, partner).wait_recv()
        total[band] += dense_in[steps - 2, band].astype(jnp.float32)

        @pl.loop(0, outers - 1)
        def _(turn):
            line_copy(2 * turn + 1, band, mirror(turn + 1)).wait_recv()
            total[band] += dense_in[2 * turn + 1, band].astype(jnp.float32)

        result = total[band]
        remapped_ref[band] = result.astype(jnp.bfloat16)
        local_sum[band] = lax.dot_general(
            mix,
            result,
            (((1,), (1,)), ((), ())),
            precision=lax.Precision.HIGHEST,
            preferred_element_type=jnp.float32,
        )
        swap(band).start()

    for spot in range(PLANE - 1):
        tag_copy(spot).wait_send()

    @pl.loop(0, steps)
    def _(step):
        for spot in range(PLANE - 1):
            for core in range(lev_count):
                chunk_copy(step, spot, core, lev).wait_send()
        chunk_copy(step, PLANE - 1, twin, lev).wait_send()

    @pl.loop(0, steps - 1)
    def _(step):
        for band in range(bands):
            line_copy(step, band, partner).wait_send()

    for band in range(bands):
        swap(band).wait()
        sum_ref[:, band * BAND:(band + 1) * BAND] = local_sum[band] + other_sum[band]


def remap(count, capacity, lev_count, level_count, cells, order, start, level, recon, weight, tags):
    columns = recon.shape[3]
    blocks = cells.shape[0]
    steps = count // PLANE
    rows = capacity * TB
    smem = pl.BlockSpec(memory_space=pltpu.SMEM)
    vmem = pl.BlockSpec(memory_space=pltpu.VMEM)
    dma = pltpu.SemaphoreType.DMA
    chunk = (lev_count, rows, columns)
    bands = T_DEV // BAND
    dense = (bands, BAND, columns)
    return pl.pallas_call(
        functools.partial(remap_kernel, count, capacity, level_count, lev_count),
        out_shape=(
            jax.ShapeDtypeStruct(dense, jnp.bfloat16),
            jax.ShapeDtypeStruct((FIELDS, T_DEV), jnp.float32),
        ),
        in_specs=[smem] * 4 + [vmem] * 3,
        out_specs=(vmem, vmem),
        scratch_shapes=[
            pltpu.VMEM((UNROLL, lev_count, 3 * SPAN, columns), jnp.float32),
            pltpu.VMEM((lev_count, -(-(blocks + capacity) // SUB) * SUB, TB, columns), jnp.bfloat16),
            pltpu.VMEM((steps, PLANE) + chunk, jnp.bfloat16),
            pltpu.VMEM((steps, PLANE) + chunk, jnp.bfloat16),
            pltpu.VMEM((PLANE, steps, SUB, LANES), jnp.int32),
            pltpu.VMEM(dense, jnp.float32),
            pltpu.VMEM((steps - 1,) + dense, jnp.bfloat16),
            pltpu.VMEM((steps - 1,) + dense, jnp.bfloat16),
            pltpu.VMEM((bands, FIELDS, BAND), jnp.float32),
            pltpu.VMEM((bands, FIELDS, BAND), jnp.float32),
            dma((steps, PLANE, lev_count)),
            dma((steps, PLANE, lev_count)),
            dma((PLANE - 1,)),
            dma((PLANE - 1,)),
            dma((steps - 1, bands)),
            dma((steps - 1, bands)),
            dma((bands,)),
            dma((bands,)),
        ],
        compiler_params=pltpu.CompilerParams(
            vmem_limit_bytes=(16 << 20) + steps * (3 << 18), collective_id=0, has_side_effects=True
        ),
        name="remap",
    )(cells, order, start, level, recon, weight, tags)


def shards(field, grad_coef, neighbours, level_weight, src_index, tgt_index, block_dest, weights):
    count = lax.axis_size("src")
    columns = field.shape[1]
    blocks = src_index.shape[0]
    lev_count = lax.axis_size("lev")
    capacity = 2 * blocks // count // lev_count
    lines = -(-capacity // GROUP)
    steps = count // PLANE
    shaped = weights.reshape(blocks, 3 * SB * TB // LANES, LANES)
    recon, order, start, tags, cells = prepare(
        count, lev_count, lines, field, grad_coef, neighbours.T, block_dest.T, tgt_index.T,
        src_index.T,
    )
    remapped, sums = remap(
        count, capacity, lev_count, columns // FIELDS, cells, order, start,
        level_weight, recon.reshape(lev_count, -1, SUB, columns), shaped, tags.reshape(PLANE, steps, SUB, LANES),
    )
    return remapped.reshape(T_DEV, columns), sums


def solution(mesh):
    placed = (
        P("src", "lev"),
        P(None, None, "src"),
        P("src", None),
        P(),
        P("src", None),
        P("src", None),
        P("src", None),
        P("src", None),
    )
    return jax.shard_map(
        shards,
        mesh=mesh,
        in_specs=placed,
        out_specs=(P("src", "lev"), P(None, "src")),
        check_vma=False,
    )
```
